32 devices in a mesh: groups: 2 (over y), ctx: 4 (over z), head: 2 (over x), aux: 2 (over core).
Axes of the slice: x: 2, y: 2, z: 4, core: 2. Of those that a mesh axis runs over, the one named last changes fastest.
Arguments:
- query_rows: bfloat16 [4096, 16, 128], P(('groups', 'ctx'), ('head', 'aux')), parts along dimension 0, may hold values from -6 to 6
- key_rows: bfloat16 [4096, 16, 128], P(('groups', 'ctx'), ('head', 'aux')), parts along dimension 0, may hold values from -6 to 6
- value_rows: bfloat16 [4096, 16, 128], P(('groups', 'ctx'), ('head', 'aux')), parts along dimension 0, may hold values from -6 to 6
- out_grad: bfloat16 [4096, 16, 128], P(('groups', 'ctx'), ('head', 'aux')), parts along dimension 0, may hold values from -6 to 6
- head_band: int32 [16, 8], P(('head', 'aux')), may hold values from 0 to 1, as said below
- frame_map: int32 [8], replicated, may hold values from 0 to 7, each once
Outputs:
- attended: bfloat16 [4096, 16, 128], P(('groups', 'ctx'), ('head', 'aux')), parts along dimension 0
- query_grad: bfloat16 [4096, 16, 128], P(('groups', 'ctx'), ('head', 'aux')), parts along dimension 0
- key_grad: bfloat16 [4096, 16, 128], P(('groups', 'ctx'), ('head', 'aux')), parts along dimension 0
- value_grad: bfloat16 [4096, 16, 128], P(('groups', 'ctx'), ('head', 'aux')), parts along dimension 0
The draws below stay inside these ranges and needn't reach their ends.
There are 2 independent parts, one for each index of `groups`. The reference program is written for one: setup_inputs(seed, part) draws one part's arguments, and reference() takes and returns one part's arrays. A program takes and returns all parts, laid end to end along the dimension named above; an argument that names none is the same for every part. Nothing has to cross between parts.
Inputs may be any that keep to these rules, and one draw needn't show every extreme that they name: head_band[h, 0] is 1 for every head. Rows r * 256 to (r + 1) * 256 - 1 of the token arrays belong to frame frame_map[r]; each frame appears once.
All inputs are finite; a program needn't handle non-finite values.
Results may differ from the reference program's by a relative error of at most 0.0095.
Values may be sent and summed in bfloat16 or wider, within the bound.
No kernel may reach another device: no remote copies, remote signals or barrier semaphores. Data moves between devices by JAX's collectives and lax.ppermute only.
A program may use at most 64 MiB of HBM per device.

```python
import jax
import jax.numpy as jnp
from jax import lax

HEAD_DIM = 128
HEADS = 16
FRAME_TOK = 256
FRAMES = 8
TOKENS = 2048
N_CTX = 4


def paired_rows(key):
    base_key = jax.random.fold_in(key, 11)
    first_key, second_key = jax.random.split(base_key, 2)
    shape_all = (TOKENS, HEADS, HEAD_DIM)
    queries = jax.random.truncated_normal(first_key, -6.0, 6.0, shape_all, jnp.float32)
    keyset = jax.random.truncated_normal(second_key, -6.0, 6.0, shape_all, jnp.float32)
    return (queries, keyset)


def draw_query_rows(key, part):
    return paired_rows(key)[0].astype(jnp.bfloat16)


def draw_key_rows(key, part):
    return paired_rows(key)[1].astype(jnp.bfloat16)


def draw_head_band(key, part):
    reach_key, extra_key = jax.random.split(jax.random.fold_in(key, 5))
    reach = jax.random.randint(reach_key, (HEADS, 1), 1, 5)
    distance = jnp.arange(FRAMES, dtype=jnp.int32)[None, :]
    level = jnp.zeros((1, FRAMES), jnp.int32)
    for power in range(1, 12):
        level = level + (distance >= 1 << power).astype(jnp.int32)
    limit = jnp.right_shift(jnp.full((1, FRAMES), 1 << 20, jnp.int32), level)
    ticket = jax.random.randint(extra_key, (HEADS, FRAMES), 0, 1 << 20)
    extra = ticket < limit
    return ((distance <= reach) | extra).astype(jnp.int32)


def levels(own_key, shape, cuts, least, high):
    level, own = 1.0, jax.random.fold_in(own_key, 6)
    for axis_at, blocks in cuts:
        heights = jnp.exp(jax.random.uniform(jax.random.fold_in(own, axis_at), (blocks,), jnp.float32, least / len(cuts), high / len(cuts)))
        level = level * jnp.repeat(heights, shape[axis_at] // blocks).reshape([-1 if axis == axis_at else 1 for axis in range(len(shape))])
    return level


def scatter_about(stream_key, dims, scale, most, pieces=(), kind=jnp.bfloat16):
    array = scale * jax.random.normal(stream_key, dims, jnp.float32)
    if pieces:
        array = array * levels(stream_key, dims, pieces, -0.22, 0.18)
    return jnp.clip(array, -most, most).astype(kind)


def setup_inputs(seed: int = 0, part: int = 0) -> dict:
    streams_of = jax.random.split(jax.random.key(seed), 7)
    part_splits = jax.random.split(jax.random.fold_in(streams_of[6], part), 7)
    return {
        "query_rows": draw_query_rows(jax.random.fold_in(jax.random.fold_in(streams_of[6], part), 71), part),
        "key_rows": draw_key_rows(jax.random.fold_in(jax.random.fold_in(streams_of[6], part), 71), part),
        "value_rows": scatter_about(part_splits[2], (TOKENS, HEADS, HEAD_DIM), 1.0, 6.0, ((0, 4), (1, 4))),
        "out_grad": scatter_about(part_splits[3], (TOKENS, HEADS, HEAD_DIM), 1.0, 6.0, ((0, 4), (1, 4))),
        "head_band": draw_head_band(jax.random.fold_in(streams_of[6], 71), part),
        "frame_map": jax.random.permutation(streams_of[5], FRAMES).astype(jnp.int32),
    }


def round_trip(values):
    narrow = lax.optimization_barrier(values.astype(jnp.bfloat16))
    return narrow.astype(jnp.float32)


def head_pass(inputs, frame_map):
    queries, keys_head, values_head, grad_rows, band_row = inputs
    scaling = HEAD_DIM ** -0.5
    frame_gap = jnp.abs(frame_map[:, None] - frame_map[None, :]).astype(jnp.int32)
    frame_ok = jnp.take(band_row, frame_gap) == 1
    block_rows = TOKENS // N_CTX
    block_frames = block_rows // FRAME_TOK

    def one_block(sums, block_id):
        first_row = (block_id * block_rows).astype(jnp.int32)
        query_block = lax.dynamic_slice_in_dim(queries, first_row, block_rows, 0)
        grad_block = lax.dynamic_slice_in_dim(grad_rows, first_row, block_rows, 0)
        frame_block = lax.dynamic_slice_in_dim(frame_ok, (block_id * block_frames).astype(jnp.int32), block_frames, 0)
        token_ok = jnp.repeat(jnp.repeat(frame_block, FRAME_TOK, axis=0), FRAME_TOK, axis=1)
        scores = jnp.dot(query_block, keys_head.T, preferred_element_type=jnp.float32) * scaling
        scores = jnp.where(token_ok, scores, -jnp.inf)
        row_max = jnp.max(scores, axis=1)
        shifted = jnp.exp(scores - row_max[:, None])
        total = jnp.sum(shifted, axis=1)
        log_total = row_max + jnp.log(total)
        out_full = jnp.dot(shifted.astype(jnp.bfloat16), values_head, preferred_element_type=jnp.float32) / total[:, None]
        row_delta = jnp.sum(grad_block.astype(jnp.float32) * out_full, axis=1)
        probabilities = jnp.exp(scores - log_total[:, None])
        value_part = jnp.dot(probabilities.astype(jnp.bfloat16).T, grad_block, preferred_element_type=jnp.float32)
        prob_grad = jnp.dot(grad_block, values_head.T, preferred_element_type=jnp.float32)
        score_grad = (probabilities * (prob_grad - row_delta[:, None])).astype(jnp.bfloat16)
        query_grad = (scaling * jnp.dot(score_grad, keys_head, preferred_element_type=jnp.float32)).astype(jnp.bfloat16)
        key_part = scaling * jnp.dot(score_grad.T, query_block, preferred_element_type=jnp.float32)
        sums = (sums[0] + round_trip(key_part), sums[1] + round_trip(value_part))
        return sums, (out_full.astype(jnp.bfloat16), query_grad)

    empty_sum = jnp.zeros((TOKENS, HEAD_DIM), jnp.float32)
    sums, outputs = lax.scan(one_block, (empty_sum, empty_sum), jnp.arange(N_CTX, dtype=jnp.int32))
    attended = outputs[0].reshape(TOKENS, HEAD_DIM)
    query_grad = outputs[1].reshape(TOKENS, HEAD_DIM)
    return attended, query_grad, sums[0].astype(jnp.bfloat16), sums[1].astype(jnp.bfloat16)


def reference(query_rows, key_rows, value_rows, out_grad, head_band, frame_map):
    per_head = (jnp.transpose(query_rows, (1, 0, 2)), jnp.transpose(key_rows, (1, 0, 2)),
                jnp.transpose(value_rows, (1, 0, 2)), jnp.transpose(out_grad, (1, 0, 2)), head_band)
    results = lax.map(lambda inputs: head_pass(inputs, frame_map), per_head)
    return (jnp.transpose(results[0], (1, 0, 2)), jnp.transpose(results[1], (1, 0, 2)),
            jnp.transpose(results[2], (1, 0, 2)), jnp.transpose(results[3], (1, 0, 2)))
```

```python
import functools
import math

import jax
import jax.numpy as jnp
from jax import lax
from jax.experimental import pallas as pl
from jax.experimental.pallas import tpu as pltpu
from jax.sharding import PartitionSpec as P

FRAME_TOK = 256


def narrowed(values):
    narrow = lax.optimization_barrier(values.astype(jnp.bfloat16))
    return narrow.astype(jnp.float32)


def keep_same(carried):
    return carried


def shard_frames(frame_map, shard_id, frame_count):
    return lax.dynamic_slice_in_dim(frame_map, shard_id * frame_count, frame_count)


def frame_allowed(band_rows, query_frames, key_frames):
    distance = jnp.abs(query_frames[:, None] - key_frames[None, :])
    offsets = jnp.arange(band_rows.shape[1], dtype=jnp.int32)
    matches = (distance[:, :, None] == offsets[None, None, :]).astype(jnp.int32)
    allowed_sum = jnp.sum(matches[None, :, :, :] * band_rows[:, None, None, :], axis=3)
    return allowed_sum > 0


def tile_scores(queries, keys_part, allowed, scaling):
    products = (
        jnp.einsum("qhd,khd->hqk", queries, keys_part, preferred_element_type=jnp.float32) * scaling
    )
    head_count, query_count, key_count = products.shape
    shaped = products.reshape(head_count, allowed.shape[1], FRAME_TOK, allowed.shape[2], FRAME_TOK)
    masked = jnp.where(allowed[:, :, None, :, None], shaped, -jnp.inf)
    return masked.reshape(head_count, query_count, key_count)


def forward_tile(carried, queries, keys_part, values_part, allowed, scaling):
    run_max, run_sum, weighted = carried
    scores = tile_scores(queries, keys_part, allowed, scaling)
    new_max = jnp.maximum(run_max, jnp.max(scores, axis=2))
    weights = jnp.exp(scores - new_max[:, :, None])
    factor = jnp.exp(run_max - new_max)
    run_sum = run_sum * factor + jnp.sum(weights, axis=2)
    update = jnp.einsum(
        "hqk,khd->qhd",
        weights.astype(jnp.bfloat16),
        values_part,
        preferred_element_type=jnp.float32,
    )
    weighted = weighted * factor.T[:, :, None] + update
    return (new_max, run_sum, weighted)


def query_grad_term(
    queries, grad_rows, log_total, row_delta, keys_part, values_part, allowed, scaling
):
    scores = tile_scores(queries, keys_part, allowed, scaling)
    probabilities = jnp.exp(scores - log_total[:, :, None])
    prob_grad = jnp.einsum(
        "qhd,khd->hqk", grad_rows, values_part, preferred_element_type=jnp.float32
    )
    score_grad = (probabilities * (prob_grad - row_delta[:, :, None])).astype(jnp.bfloat16)
    return jnp.einsum("hqk,khd->qhd", score_grad, keys_part, preferred_element_type=jnp.float32)


def key_grad_terms(
    queries, grad_rows, log_total, row_delta, keys_part, values_part, allowed, scaling
):
    scores = tile_scores(queries, keys_part, allowed, scaling)
    probabilities = jnp.exp(scores - log_total[:, :, None])
    value_term = jnp.einsum(
        "hqk,qhd->khd",
        probabilities.astype(jnp.bfloat16),
        grad_rows,
        preferred_element_type=jnp.float32,
    )
    prob_grad = jnp.einsum(
        "qhd,khd->hqk", grad_rows, values_part, preferred_element_type=jnp.float32
    )
    score_grad = (probabilities * (prob_grad - row_delta[:, :, None])).astype(jnp.bfloat16)
    key_term = scaling * jnp.einsum(
        "hqk,qhd->khd", score_grad, queries, preferred_element_type=jnp.float32
    )
    return (key_term, value_term)


def shard_scan(step, carried, pieces, shard_rows):
    shard_total = pieces[0].shape[0] // shard_rows
    stacked = tuple(
        (member.reshape((shard_total, shard_rows) + member.shape[1:]) for member in pieces)
    )
    shard_ids = jnp.arange(shard_total, dtype=jnp.int32)

    def advance(current, element):
        return (step(current, element[1], element[0]), None)

    result, unused_out = lax.scan(advance, carried, (shard_ids, stacked))
    return result


def gather_plan(query_rows, key_rows, value_rows, out_grad, head_band, frame_map):
    shard_rows = query_rows.shape[0]
    head_count = query_rows.shape[1]
    head_width = query_rows.shape[2]
    frame_count = shard_rows // FRAME_TOK
    scaling = head_width ** (-0.5)
    own_index = lax.axis_index("ctx")
    own_frames = shard_frames(frame_map, own_index, frame_count)
    all_keys = lax.all_gather(key_rows, "ctx", axis=0, tiled=True)
    all_values = lax.all_gather(value_rows, "ctx", axis=0, tiled=True)

    def forward_step(carried, pieces, shard_id):
        allowed = frame_allowed(
            head_band, own_frames, shard_frames(frame_map, shard_id, frame_count)
        )

        def forward_compute(current):
            return forward_tile(current, query_rows, pieces[0], pieces[1], allowed, scaling)

        return lax.cond(jnp.any(allowed), forward_compute, keep_same, carried)

    start_state = (
        jnp.full((head_count, shard_rows), -1e30, jnp.float32),
        jnp.zeros((head_count, shard_rows), jnp.float32),
        jnp.zeros((shard_rows, head_count, head_width), jnp.float32),
    )
    forward_state = shard_scan(forward_step, start_state, (all_keys, all_values), shard_rows)
    run_max, run_sum, weighted = forward_state
    out_full = weighted / run_sum.T[:, :, None]
    attended = out_full.astype(jnp.bfloat16)
    log_total = run_max + jnp.log(run_sum)
    row_delta = jnp.sum(out_grad.astype(jnp.float32) * out_full, axis=2).T
    zero_rows = jnp.zeros((shard_rows, head_count, head_width), jnp.float32)

    def backward_step(carried, pieces, shard_id):
        allowed = frame_allowed(
            head_band, own_frames, shard_frames(frame_map, shard_id, frame_count)
        )

        def backward_compute(current):
            return current + query_grad_term(
                query_rows, out_grad, log_total, row_delta, pieces[0], pieces[1], allowed, scaling
            )

        return lax.cond(jnp.any(allowed), backward_compute, keep_same, carried)

    query_sum = shard_scan(backward_step, zero_rows, (all_keys, all_values), shard_rows)
    query_grad = (scaling * query_sum).astype(jnp.bfloat16)
    all_stats = (
        lax.all_gather(log_total, "ctx", axis=1, tiled=True),
        lax.all_gather(row_delta, "ctx", axis=1, tiled=True),
    )

    def key_step(carried, pieces, shard_id):
        allowed = frame_allowed(
            head_band, shard_frames(frame_map, shard_id, frame_count), own_frames
        )
        stat_log = lax.dynamic_slice_in_dim(all_stats[0], shard_id * shard_rows, shard_rows, 1)
        stat_delta = lax.dynamic_slice_in_dim(all_stats[1], shard_id * shard_rows, shard_rows, 1)

        def key_compute(current):
            key_term, value_term = key_grad_terms(
                pieces[0], pieces[1], stat_log, stat_delta, key_rows, value_rows, allowed, scaling
            )
            return (current[0] + narrowed(key_term), current[1] + narrowed(value_term))

        return lax.cond(jnp.any(allowed), key_compute, keep_same, carried)

    key_sum, value_sum = shard_scan(
        key_step,
        (zero_rows, zero_rows),
        (
            lax.all_gather(query_rows, "ctx", axis=0, tiled=True),
            lax.all_gather(out_grad, "ctx", axis=0, tiled=True),
        ),
        shard_rows,
    )
    key_grad = key_sum.astype(jnp.bfloat16)
    value_grad = value_sum.astype(jnp.bfloat16)
    return (attended, query_grad, key_grad, value_grad)


VMEM = pl.BlockSpec(memory_space=pltpu.VMEM)
SMEM = pl.BlockSpec(memory_space=pltpu.SMEM)


def spread_body(slots, own_ref, first_ref, second_ref, *rest):
    outs, wide = rest[:slots], rest[slots]
    width = first_ref.shape[1]
    tokens = first_ref.shape[0] // slots
    own = own_ref[0]
    for part, source in enumerate((first_ref, second_ref)):
        wide[...] = source[...].astype(jnp.float32)
        for slot in range(slots):
            picked = wide[pl.ds(own ^ slot, tokens, stride=slots), :]
            outs[slot][:, part * width : (part + 1) * width] = picked.astype(jnp.bfloat16)


def spread(own, first, second):
    tokens, slots, width = first.shape
    rows = tokens * slots
    return pl.pallas_call(
        functools.partial(spread_body, slots),
        out_shape=[jax.ShapeDtypeStruct((tokens, 2 * width), jnp.bfloat16)] * slots,
        in_specs=[SMEM, VMEM, VMEM],
        out_specs=[VMEM] * slots,
        scratch_shapes=[pltpu.VMEM((rows, width), jnp.float32)],
        cost_estimate=pl.CostEstimate(flops=0, transcendentals=0, bytes_accessed=8 * rows * width),
        name="spread",
    )(own, first.reshape(rows, width), second.reshape(rows, width))


def collect_body(slots, own_ref, *rest):
    pieces, (first_ref, second_ref, wide) = rest[:slots], rest[slots:]
    width = first_ref.shape[1]
    tokens = first_ref.shape[0] // slots
    own = own_ref[0]
    for part, target in enumerate((first_ref, second_ref)):
        for slot in range(slots):
            piece = pieces[slot][:, part * width : (part + 1) * width]
            wide[pl.ds(own ^ slot, tokens, stride=slots), :] = piece.astype(jnp.float32)
        target[...] = wide[...].astype(jnp.bfloat16)


def collect(own, pieces):
    slots = len(pieces)
    tokens, width = pieces[0].shape[0], pieces[0].shape[1] // 2
    rows = tokens * slots
    first, second = pl.pallas_call(
        functools.partial(collect_body, slots),
        out_shape=[jax.ShapeDtypeStruct((rows, width), jnp.bfloat16)] * 2,
        in_specs=[SMEM] + [VMEM] * slots,
        out_specs=[VMEM] * 2,
        scratch_shapes=[pltpu.VMEM((rows, width), jnp.float32)],
        cost_estimate=pl.CostEstimate(flops=0, transcendentals=0, bytes_accessed=8 * rows * width),
        name="collect",
    )(own, *pieces)
    return first.reshape(tokens, slots, width), second.reshape(tokens, slots, width)


def join_body(slots, *refs):
    pieces, (rows_ref, flat_ref) = refs[:slots], refs[slots:]
    tokens = pieces[0].shape[0]
    for slot in range(slots):
        piece = pieces[slot][...]
        rows_ref[slot * tokens : (slot + 1) * tokens, :] = piece
        flat_ref[:, slot * tokens : (slot + 1) * tokens] = piece.T


def join(pieces):
    slots = len(pieces)
    tokens, both = pieces[0].shape
    return pl.pallas_call(
        functools.partial(join_body, slots),
        out_shape=[
            jax.ShapeDtypeStruct((slots * tokens, both), jnp.bfloat16),
            jax.ShapeDtypeStruct((both, slots * tokens), jnp.bfloat16),
        ],
        in_specs=[VMEM] * slots,
        out_specs=[VMEM] * 2,
        cost_estimate=pl.CostEstimate(
            flops=0, transcendentals=0, bytes_accessed=6 * slots * tokens * both
        ),
        name="join",
    )(*pieces)


def attend_body(
    slots, slot, first, last, own_ref, band_ref, map_ref, qg_ref, kv_ref, kvt_ref, *rest
):
    if first:
        sums_in = None
    else:
        sums_in, rest = rest[0], rest[1:]
    out_ref, rest = rest[0], rest[1:]
    if last:
        parts, rest = rest[:slots], rest[slots:]
        sums_ref, rest = rest[0], rest[1:]
    else:
        sums_ref, rest = rest[0], rest[1:]
    scores_ref, out_acc, grad_acc = rest
    tokens = qg_ref.shape[0]
    width = qg_ref.shape[1] // 2
    frames = tokens // FRAME_TOK
    keys = kv_ref.shape[0]
    scaling = width ** (-0.5)
    power = scaling * math.log2(math.e)
    own = own_ref[0]

    queries = qg_ref[:, :width]
    grads = qg_ref[:, width:]
    queries_t = queries.T
    grads_t = grads.T
    lane = lax.broadcasted_iota(jnp.int32, (1, tokens), 1)

    def allowed_row(tile):
        key_frame = map_ref[(own ^ (tile // frames)) * frames + tile % frames]
        row = jnp.zeros((1, tokens), jnp.int32)
        for frame in range(frames):
            gap = jnp.abs(map_ref[(own ^ slot) * frames + frame] - key_frame)
            row = jnp.where(lane // FRAME_TOK == frame, band_ref[own, gap], row)
        return row == 1

    def tile_rows(tile):
        return pl.ds(pl.multiple_of(tile * FRAME_TOK, FRAME_TOK), FRAME_TOK)

    def score_step(tile, row_max):
        rows = tile_rows(tile)
        scores = jnp.dot(kv_ref[rows, :width], queries_t, preferred_element_type=jnp.float32)
        scores_ref[rows, :] = scores
        tile_max = jnp.max(scores, axis=0, keepdims=True)
        return jnp.maximum(row_max, jnp.where(allowed_row(tile), tile_max, -jnp.inf))

    tiles = keys // FRAME_TOK
    row_max = lax.fori_loop(0, tiles, score_step, jnp.full((1, tokens), -jnp.inf, jnp.float32))
    row_max = row_max * power
    out_acc[...] = jnp.zeros_like(out_acc)

    def weight_step(tile, total):
        rows = tile_rows(tile)
        shift = jnp.where(allowed_row(tile), row_max, jnp.inf)
        weights = jnp.exp2(scores_ref[rows, :] * power - shift)
        scores_ref[rows, :] = weights
        out_acc[...] += jnp.dot(
            kvt_ref[width:, rows], weights.astype(jnp.bfloat16), preferred_element_type=jnp.float32
        )
        return total + jnp.sum(weights, axis=0, keepdims=True)

    total = lax.fori_loop(0, tiles, weight_step, jnp.zeros((1, tokens), jnp.float32))
    inverse = 1.0 / total
    out_full = out_acc[...] * inverse
    delta = jnp.sum(out_full * grads_t.astype(jnp.float32), axis=0, keepdims=True)
    out_ref[:, :width] = out_full.T.astype(jnp.bfloat16)
    grad_acc[...] = jnp.zeros_like(grad_acc)

    def grad_step(tile, carried):
        rows = tile_rows(tile)
        probabilities = scores_ref[rows, :] * inverse
        prob_grad = jnp.dot(kv_ref[rows, width:], grads_t, preferred_element_type=jnp.float32)
        score_grad = (probabilities * (prob_grad - delta)).astype(jnp.bfloat16)
        value_term = jnp.dot(
            probabilities.astype(jnp.bfloat16), grads, preferred_element_type=jnp.float32
        )
        key_term = jnp.dot(score_grad, queries, preferred_element_type=jnp.float32)
        grad_acc[...] += jnp.dot(
            kvt_ref[:width, rows], score_grad, preferred_element_type=jnp.float32
        )
        if first:
            sums_ref[rows, :width] = key_term
            sums_ref[rows, width:] = value_term
        else:
            sums_ref[rows, :width] = sums_in[rows, :width] + key_term
            sums_ref[rows, width:] = sums_in[rows, width:] + value_term
        return carried

    lax.fori_loop(0, tiles, grad_step, 0)
    out_ref[:, width:] = (grad_acc[...] * scaling).T.astype(jnp.bfloat16)
    if last:
        for part in range(slots):
            rows = slice(part * tokens, (part + 1) * tokens)
            parts[part][:, :width] = (sums_ref[rows, :width] * scaling).astype(jnp.bfloat16)
            parts[part][:, width:] = sums_ref[rows, width:].astype(jnp.bfloat16)


def attend(slots, slot, first, last, own, head_band, frame_map, pair, kv, kvt, sums):
    tokens, both = pair.shape
    keys, width = kv.shape[0], both // 2
    piece = jax.ShapeDtypeStruct((tokens, both), jnp.bfloat16)
    sums_shape = jax.ShapeDtypeStruct((keys, both), jnp.float32)
    outs = [piece] + ([piece] * slots if last else [sums_shape])
    scratch = [
        pltpu.VMEM((keys, tokens), jnp.float32),
        pltpu.VMEM((width, tokens), jnp.float32),
        pltpu.VMEM((width, tokens), jnp.float32),
    ]
    if last:
        scratch = [pltpu.VMEM((keys, both), jnp.float32)] + scratch
    operands = [own, head_band, frame_map, pair, kv, kvt] + ([] if first else [sums])
    return pl.pallas_call(
        functools.partial(attend_body, slots, slot, first, last),
        out_shape=outs,
        in_specs=[SMEM] * 3 + [VMEM] * (len(operands) - 3),
        out_specs=[VMEM] * len(outs),
        scratch_shapes=scratch,
        input_output_aliases={} if first or last else {6: 1},
        cost_estimate=pl.CostEstimate(
            flops=12 * tokens * keys * width,
            transcendentals=tokens * keys,
            bytes_accessed=10 * keys * both,
        ),
        name="attend",
    )(*operands)


def exchange_plan(slots, query_rows, key_rows, value_rows, out_grad, head_band, frame_map):
    own_index = lax.axis_index("ctx").astype(jnp.int32)
    own = own_index.reshape(1)

    def swap(piece, slot):
        return lax.ppermute(piece, "ctx", [(place, place ^ slot) for place in range(slots)])

    kv_pieces = spread(own, key_rows, value_rows)
    qg_pieces = spread(own, query_rows, out_grad)
    kv_slots = [kv_pieces[0]] + [swap(kv_pieces[slot], slot) for slot in range(1, slots)]
    qg_slots = [qg_pieces[0]] + [swap(qg_pieces[slot], slot) for slot in range(1, slots)]
    kv, kvt = join(kv_slots)
    out_pieces = []
    sums = None
    for slot in range(slots):
        last = slot == slots - 1
        results = attend(
            slots, slot, slot == 0, last, own, head_band, frame_map, qg_slots[slot], kv, kvt, sums
        )
        out_pieces.append(results[0])
        sums = results[1]
    grad_pieces = results[1:]
    out_back = [out_pieces[0]] + [swap(out_pieces[slot], slot) for slot in range(1, slots)]
    grad_back = [grad_pieces[0]] + [swap(grad_pieces[slot], slot) for slot in range(1, slots)]
    attended, query_grad = collect(own, out_back)
    key_grad, value_grad = collect(own, grad_back)
    return (attended, query_grad, key_grad, value_grad)


def solution(mesh):
    slots = mesh.shape["ctx"]

    def on_device(query_rows, *others):
        if query_rows.shape[1] == slots and slots & (slots - 1) == 0:
            return exchange_plan(slots, query_rows, *others)
        return gather_plan(query_rows, *others)

    rows = P(("groups", "ctx"), ("head", "aux"), None)
    return jax.shard_map(
        on_device,
        mesh=mesh,
        in_specs=(rows, rows, rows, rows, P(("head", "aux"), None), P()),
        out_specs=(rows, rows, rows, rows),
        check_vma=False,
    )
```

```python
import functools
import math

import jax
import jax.numpy as jnp
from jax import lax
from jax.experimental import pallas as pl
from jax.experimental.pallas import tpu as pltpu
from jax.sharding import PartitionSpec as P

FRAME_TOK = 256


def narrowed(values):
    narrow = lax.optimization_barrier(values.astype(jnp.bfloat16))
    return narrow.astype(jnp.float32)


def keep_same(carried):
    return carried


def shard_frames(frame_map, shard_id, frame_count):
    return lax.dynamic_slice_in_dim(frame_map, shard_id * frame_count, frame_count)


def frame_allowed(band_rows, query_frames, key_frames):
    distance = jnp.abs(query_frames[:, None] - key_frames[None, :])
    offsets = jnp.arange(band_rows.shape[1], dtype=jnp.int32)
    matches = (distance[:, :, None] == offsets[None, None, :]).astype(jnp.int32)
    allowed_sum = jnp.sum(matches[None, :, :, :] * band_rows[:, None, None, :], axis=3)
    return allowed_sum > 0


def tile_scores(queries, keys_part, allowed, scaling):
    products = (
        jnp.einsum("qhd,khd->hqk", queries, keys_part, preferred_element_type=jnp.float32) * scaling
    )
    head_count, query_count, key_count = products.shape
    shaped = products.reshape(head_count, allowed.shape[1], FRAME_TOK, allowed.shape[2], FRAME_TOK)
    masked = jnp.where(allowed[:, :, None, :, None], shaped, -jnp.inf)
    return masked.reshape(head_count, query_count, key_count)


def forward_tile(carried, queries, keys_part, values_part, allowed, scaling):
    run_max, run_sum, weighted = carried
    scores = tile_scores(queries, keys_part, allowed, scaling)
    new_max = jnp.maximum(run_max, jnp.max(scores, axis=2))
    weights = jnp.exp(scores - new_max[:, :, None])
    factor = jnp.exp(run_max - new_max)
    run_sum = run_sum * factor + jnp.sum(weights, axis=2)
    update = jnp.einsum(
        "hqk,khd->qhd",
        weights.astype(jnp.bfloat16),
        values_part,
        preferred_element_type=jnp.float32,
    )
    weighted = weighted * factor.T[:, :, None] + update
    return (new_max, run_sum, weighted)


def query_grad_term(
    queries, grad_rows, log_total, row_delta, keys_part, values_part, allowed, scaling
):
    scores = tile_scores(queries, keys_part, allowed, scaling)
    probabilities = jnp.exp(scores - log_total[:, :, None])
    prob_grad = jnp.einsum(
        "qhd,khd->hqk", grad_rows, values_part, preferred_element_type=jnp.float32
    )
    score_grad = (probabilities * (prob_grad - row_delta[:, :, None])).astype(jnp.bfloat16)
    return jnp.einsum("hqk,khd->qhd", score_grad, keys_part, preferred_element_type=jnp.float32)


def key_grad_terms(
    queries, grad_rows, log_total, row_delta, keys_part, values_part, allowed, scaling
):
    scores = tile_scores(queries, keys_part, allowed, scaling)
    probabilities = jnp.exp(scores - log_total[:, :, None])
    value_term = jnp.einsum(
        "hqk,qhd->khd",
        probabilities.astype(jnp.bfloat16),
        grad_rows,
        preferred_element_type=jnp.float32,
    )
    prob_grad = jnp.einsum(
        "qhd,khd->hqk", grad_rows, values_part, preferred_element_type=jnp.float32
    )
    score_grad = (probabilities * (prob_grad - row_delta[:, :, None])).astype(jnp.bfloat16)
    key_term = scaling * jnp.einsum(
        "hqk,qhd->khd", score_grad, queries, preferred_element_type=jnp.float32
    )
    return (key_term, value_term)


def shard_scan(step, carried, pieces, shard_rows):
    shard_total = pieces[0].shape[0] // shard_rows
    stacked = tuple(
        (member.reshape((shard_total, shard_rows) + member.shape[1:]) for member in pieces)
    )
    shard_ids = jnp.arange(shard_total, dtype=jnp.int32)

    def advance(current, element):
        return (step(current, element[1], element[0]), None)

    result, unused_out = lax.scan(advance, carried, (shard_ids, stacked))
    return result


def gather_plan(query_rows, key_rows, value_rows, out_grad, head_band, frame_map):
    shard_rows = query_rows.shape[0]
    head_count = query_rows.shape[1]
    head_width = query_rows.shape[2]
    frame_count = shard_rows // FRAME_TOK
    scaling = head_width ** (-0.5)
    own_index = lax.axis_index("ctx")
    own_frames = shard_frames(frame_map, own_index, frame_count)
    all_keys = lax.all_gather(key_rows, "ctx", axis=0, tiled=True)
    all_values = lax.all_gather(value_rows, "ctx", axis=0, tiled=True)

    def forward_step(carried, pieces, shard_id):
        allowed = frame_allowed(
            head_band, own_frames, shard_frames(frame_map, shard_id, frame_count)
        )

        def forward_compute(current):
            return forward_tile(current, query_rows, pieces[0], pieces[1], allowed, scaling)

        return lax.cond(jnp.any(allowed), forward_compute, keep_same, carried)

    start_state = (
        jnp.full((head_count, shard_rows), -1e30, jnp.float32),
        jnp.zeros((head_count, shard_rows), jnp.float32),
        jnp.zeros((shard_rows, head_count, head_width), jnp.float32),
    )
    forward_state = shard_scan(forward_step, start_state, (all_keys, all_values), shard_rows)
    run_max, run_sum, weighted = forward_state
    out_full = weighted / run_sum.T[:, :, None]
    attended = out_full.astype(jnp.bfloat16)
    log_total = run_max + jnp.log(run_sum)
    row_delta = jnp.sum(out_grad.astype(jnp.float32) * out_full, axis=2).T
    zero_rows = jnp.zeros((shard_rows, head_count, head_width), jnp.float32)

    def backward_step(carried, pieces, shard_id):
        allowed = frame_allowed(
            head_band, own_frames, shard_frames(frame_map, shard_id, frame_count)
        )

        def backward_compute(current):
            return current + query_grad_term(
                query_rows, out_grad, log_total, row_delta, pieces[0], pieces[1], allowed, scaling
            )

        return lax.cond(jnp.any(allowed), backward_compute, keep_same, carried)

    query_sum = shard_scan(backward_step, zero_rows, (all_keys, all_values), shard_rows)
    query_grad = (scaling * query_sum).astype(jnp.bfloat16)
    all_stats = (
        lax.all_gather(log_total, "ctx", axis=1, tiled=True),
        lax.all_gather(row_delta, "ctx", axis=1, tiled=True),
    )

    def key_step(carried, pieces, shard_id):
        allowed = frame_allowed(
            head_band, shard_frames(frame_map, shard_id, frame_count), own_frames
        )
        stat_log = lax.dynamic_slice_in_dim(all_stats[0], shard_id * shard_rows, shard_rows, 1)
        stat_delta = lax.dynamic_slice_in_dim(all_stats[1], shard_id * shard_rows, shard_rows, 1)

        def key_compute(current):
            key_term, value_term = key_grad_terms(
                pieces[0], pieces[1], stat_log, stat_delta, key_rows, value_rows, allowed, scaling
            )
            return (current[0] + narrowed(key_term), current[1] + narrowed(value_term))

        return lax.cond(jnp.any(allowed), key_compute, keep_same, carried)

    key_sum, value_sum = shard_scan(
        key_step,
        (zero_rows, zero_rows),
        (
            lax.all_gather(query_rows, "ctx", axis=0, tiled=True),
            lax.all_gather(out_grad, "ctx", axis=0, tiled=True),
        ),
        shard_rows,
    )
    key_grad = key_sum.astype(jnp.bfloat16)
    value_grad = value_sum.astype(jnp.bfloat16)
    return (attended, query_grad, key_grad, value_grad)


VMEM = pl.BlockSpec(memory_space=pltpu.VMEM)
SMEM = pl.BlockSpec(memory_space=pltpu.SMEM)
HBM = pl.BlockSpec(memory_space=pltpu.HBM)


def spread_body(slots, chunks, own_ref, *refs):
    sources, refs = refs[:4], refs[4:]
    kv_refs, qg_refs, (stage, wide, arrived) = refs[: slots - 1], refs[slots - 1 : -3], refs[-3:]
    rows, width = sources[0].shape
    part_rows = rows // chunks
    part_tokens = part_rows // slots
    own = own_ref[0]
    copies = [
        [
            pltpu.make_async_copy(
                source.at[pl.ds(chunk * part_rows, part_rows), :],
                stage.at[which, pl.ds(chunk * part_rows, part_rows), :],
                arrived.at[which, chunk],
            )
            for chunk in range(chunks)
        ]
        for which, source in enumerate(sources)
    ]
    for array in copies:
        for copy in array:
            copy.start()
    for which, array in enumerate(copies):
        for chunk, copy in enumerate(array):
            copy.wait()
            first = chunk * part_rows
            wide[which, first : first + part_rows, :] = stage[
                which, first : first + part_rows, :
            ].astype(jnp.float32)
            tokens = slice(chunk * part_tokens, (chunk + 1) * part_tokens)
            for slot in range(slots):
                picked = wide[which, pl.ds(first + (own ^ slot), part_tokens, stride=slots), :]
                column = (which % 2) * width
                if which < 2 and slot == 1:
                    target, column = qg_refs[1], column + 2 * width
                elif which < 2:
                    target = kv_refs[max(slot - 1, 0)]
                else:
                    target = qg_refs[slot]
                target[tokens, column : column + width] = picked.astype(jnp.bfloat16)


def spread(own, keys, values, queries, grads, chunks=4):
    tokens, slots, width = keys.shape
    rows = tokens * slots
    pair = jax.ShapeDtypeStruct((tokens, 2 * width), jnp.bfloat16)
    both = jax.ShapeDtypeStruct((tokens, 4 * width), jnp.bfloat16)
    results = pl.pallas_call(
        functools.partial(spread_body, slots, chunks),
        out_shape=[pair] * (slots - 1) + [pair, both] + [pair] * (slots - 2),
        in_specs=[SMEM] + [HBM] * 4,
        out_specs=[VMEM] * (2 * slots - 1),
        scratch_shapes=[
            pltpu.VMEM((4, rows, width), jnp.bfloat16),
            pltpu.VMEM((4, rows, width), jnp.float32),
            pltpu.SemaphoreType.DMA((4, chunks)),
        ],
        cost_estimate=pl.CostEstimate(flops=0, transcendentals=0, bytes_accessed=16 * rows * width),
        compiler_params=pltpu.CompilerParams(vmem_limit_bytes=16 << 20),
        name="spread",
    )(
        own,
        *(
            pltpu.with_memory_space_constraint(array.reshape(rows, width), pltpu.HBM)
            for array in (keys, values, queries, grads)
        ),
    )
    kv, qg = list(results[: slots - 1]), list(results[slots - 1 :])
    return [kv[0], None] + kv[1:], qg


def collect_body(slots, starts, own_ref, *rest):
    pieces, (first_ref, second_ref, wide) = rest[:slots], rest[slots:]
    width = first_ref.shape[1]
    tokens = first_ref.shape[0] // slots
    own = own_ref[0]
    for part, target in enumerate((first_ref, second_ref)):
        for slot in range(slots):
            start = starts[slot] + part * width
            piece = pieces[slot][:, start : start + width]
            wide[pl.ds(own ^ slot, tokens, stride=slots), :] = piece.astype(jnp.float32)
        target[...] = wide[...].astype(jnp.bfloat16)


def collect(own, pieces, starts):
    slots = len(pieces)
    tokens, width = pieces[0].shape[0], pieces[0].shape[1] // 2
    rows = tokens * slots
    first, second = pl.pallas_call(
        functools.partial(collect_body, slots, starts),
        out_shape=[jax.ShapeDtypeStruct((rows, width), jnp.bfloat16)] * 2,
        in_specs=[SMEM] + [VMEM] * slots,
        out_specs=[VMEM] * 2,
        scratch_shapes=[pltpu.VMEM((rows, width), jnp.float32)],
        cost_estimate=pl.CostEstimate(flops=0, transcendentals=0, bytes_accessed=8 * rows * width),
        compiler_params=pltpu.CompilerParams(vmem_limit_bytes=12 << 20),
        name="collect",
    )(own, *pieces)
    return first.reshape(tokens, slots, width), second.reshape(tokens, slots, width)


def join_body(slots, *refs):
    pieces, (rows_ref, flat_ref) = refs[:slots], refs[slots:]
    tokens = pieces[0].shape[0]
    both = rows_ref.shape[1]
    for slot in range(slots):
        piece = pieces[slot][:, pieces[slot].shape[1] - both :]
        rows_ref[slot * tokens : (slot + 1) * tokens, :] = piece
        flat_ref[:, slot * tokens : (slot + 1) * tokens] = piece.T


def join(pieces):
    slots = len(pieces)
    tokens, both = pieces[0].shape
    return pl.pallas_call(
        functools.partial(join_body, slots),
        out_shape=[
            jax.ShapeDtypeStruct((slots * tokens, both), jnp.bfloat16),
            jax.ShapeDtypeStruct((both, slots * tokens), jnp.bfloat16),
        ],
        in_specs=[VMEM] * slots,
        out_specs=[VMEM] * 2,
        cost_estimate=pl.CostEstimate(
            flops=0, transcendentals=0, bytes_accessed=6 * slots * tokens * both
        ),
        compiler_params=pltpu.CompilerParams(vmem_limit_bytes=12 << 20),
        name="join",
    )(*pieces)


def attend_body(
    slots, slot, first, last, own_ref, band_ref, map_ref, qg_ref, kv_ref, kvt_ref, *rest
):
    if first:
        sums_in = None
    else:
        sums_in, rest = rest[0], rest[1:]
    if last:
        passenger, rest = rest[0], rest[1:]
    out_ref, rest = rest[0], rest[1:]
    if last:
        parts, rest = rest[:slots], rest[slots:]
        sums_ref, rest = rest[0], rest[1:]
        parts[1][:, kv_ref.shape[1] :] = passenger[...]
    else:
        sums_ref, rest = rest[0], rest[1:]
    scores_ref, out_acc, grad_acc = rest
    tokens = qg_ref.shape[0]
    width = kv_ref.shape[1] // 2
    frames = tokens // FRAME_TOK
    keys = kv_ref.shape[0]
    scaling = width ** (-0.5)
    power = scaling * math.log2(math.e)
    own = own_ref[0]

    queries = qg_ref[:, :width]
    grads = qg_ref[:, width : 2 * width]
    queries_t = queries.T
    grads_t = grads.T
    lane = lax.broadcasted_iota(jnp.int32, (1, tokens), 1)

    def allowed_row(tile):
        key_frame = map_ref[(own ^ (tile // frames)) * frames + tile % frames]
        row = jnp.zeros((1, tokens), jnp.int32)
        for frame in range(frames):
            gap = jnp.abs(map_ref[(own ^ slot) * frames + frame] - key_frame)
            row = jnp.where(lane // FRAME_TOK == frame, band_ref[own, gap], row)
        return row == 1

    def tile_rows(tile):
        return pl.ds(pl.multiple_of(tile * FRAME_TOK, FRAME_TOK), FRAME_TOK)

    def score_step(tile, row_max):
        rows = tile_rows(tile)
        scores = jnp.dot(kv_ref[rows, :width], queries_t, preferred_element_type=jnp.float32)
        scores_ref[rows, :] = scores
        tile_max = jnp.max(scores, axis=0, keepdims=True)
        return jnp.maximum(row_max, jnp.where(allowed_row(tile), tile_max, -jnp.inf))

    tiles = keys // FRAME_TOK
    row_max = lax.fori_loop(0, tiles, score_step, jnp.full((1, tokens), -jnp.inf, jnp.float32), unroll=8)
    row_max = row_max * power
    out_acc[...] = jnp.zeros_like(out_acc)

    def weight_step(tile, total):
        rows = tile_rows(tile)
        shift = jnp.where(allowed_row(tile), row_max, jnp.inf)
        weights = jnp.exp2(scores_ref[rows, :] * power - shift)
        scores_ref[rows, :] = weights
        out_acc[...] += jnp.dot(
            kvt_ref[width:, rows], weights.astype(jnp.bfloat16), preferred_element_type=jnp.float32
        )
        return total + jnp.sum(weights, axis=0, keepdims=True)

    total = lax.fori_loop(0, tiles, weight_step, jnp.zeros((1, tokens), jnp.float32), unroll=8)
    inverse = 1.0 / total
    out_full = out_acc[...] * inverse
    delta = jnp.sum(out_full * grads_t.astype(jnp.float32), axis=0, keepdims=True)
    out_ref[:, :width] = out_full.T.astype(jnp.bfloat16)
    grad_acc[...] = jnp.zeros_like(grad_acc)

    def grad_step(tile, carried):
        rows = tile_rows(tile)
        probabilities = scores_ref[rows, :] * inverse
        prob_grad = jnp.dot(kv_ref[rows, width:], grads_t, preferred_element_type=jnp.float32)
        score_grad = (probabilities * (prob_grad - delta)).astype(jnp.bfloat16)
        value_term = jnp.dot(
            probabilities.astype(jnp.bfloat16), grads, preferred_element_type=jnp.float32
        )
        key_term = jnp.dot(score_grad, queries, preferred_element_type=jnp.float32)
        grad_acc[...] += jnp.dot(
            kvt_ref[:width, rows], score_grad, preferred_element_type=jnp.float32
        )
        if first:
            sums_ref[rows, :width] = key_term
            sums_ref[rows, width:] = value_term
        else:
            sums_ref[rows, :width] = sums_in[rows, :width] + key_term
            sums_ref[rows, width:] = sums_in[rows, width:] + value_term
        return carried

    lax.fori_loop(0, tiles, grad_step, 0, unroll=8)
    out_ref[:, width:] = (grad_acc[...] * scaling).T.astype(jnp.bfloat16)
    if last:
        for part in range(slots):
            rows = slice(part * tokens, (part + 1) * tokens)
            parts[part][:, :width] = (sums_ref[rows, :width] * scaling).astype(jnp.bfloat16)
            parts[part][:, width : 2 * width] = sums_ref[rows, width:].astype(jnp.bfloat16)


def attend(slots, slot, first, last, own, head_band, frame_map, pair, kv, kvt, sums, passenger=None):
    tokens, both = pair.shape[0], kv.shape[1]
    keys, width = kv.shape[0], both // 2
    piece = jax.ShapeDtypeStruct((tokens, both), jnp.bfloat16)
    sums_shape = jax.ShapeDtypeStruct((keys, both), jnp.float32)
    outs = [piece] + ([piece] * slots if last else [sums_shape])
    if last:
        outs[2] = jax.ShapeDtypeStruct((tokens, 2 * both), jnp.bfloat16)
    scratch = [
        pltpu.VMEM((keys, tokens), jnp.float32),
        pltpu.VMEM((width, tokens), jnp.float32),
        pltpu.VMEM((width, tokens), jnp.float32),
    ]
    if last:
        scratch = [pltpu.VMEM((keys, both), jnp.float32)] + scratch
    operands = [own, head_band, frame_map, pair, kv, kvt] + ([] if first else [sums])
    if last:
        operands.append(passenger)
    return pl.pallas_call(
        functools.partial(attend_body, slots, slot, first, last),
        out_shape=outs,
        in_specs=[SMEM] * 3 + [VMEM] * (len(operands) - 3),
        out_specs=[VMEM] * len(outs),
        scratch_shapes=scratch,
        input_output_aliases={} if first or last else {6: 1},
        cost_estimate=pl.CostEstimate(
            flops=12 * tokens * keys * width,
            transcendentals=tokens * keys,
            bytes_accessed=10 * keys * both,
        ),
        compiler_params=pltpu.CompilerParams(vmem_limit_bytes=24 << 20),
        name="attend",
    )(*operands)


def exchange_plan(slots, query_rows, key_rows, value_rows, out_grad, head_band, frame_map):
    own_index = lax.axis_index("ctx").astype(jnp.int32)
    own = own_index.reshape(1)

    def swap(piece, slot):
        return lax.ppermute(piece, "ctx", [(place, place ^ slot) for place in range(slots)])

    def after(values, *gates):
        return lax.optimization_barrier((values, gates))[0]

    kv_slots, qg_slots = spread(own, key_rows, value_rows, query_rows, out_grad)
    for slot in range(2, slots):
        kv_slots[slot] = swap(kv_slots[slot], slot)
    kv_slots[1] = qg_slots[1] = swap(qg_slots[1], 1)
    kv, kvt = join(kv_slots)
    both = kv.shape[1]
    back = list(kv_slots)
    gate = kv_slots
    sums = None
    for slot in range(slots):
        last = slot == slots - 1
        if slot + 2 < slots:
            qg_slots[slot + 2] = swap(after(qg_slots[slot + 2], gate), slot + 2)
        results = attend(
            slots, slot, slot == 0, last, own, head_band, frame_map, qg_slots[slot], kv, kvt, sums,
            back[1],
        )
        back[slot] = results[0] if slot < 2 else swap(results[0], slot)
        sums = results[1]
        gate = results[0]
    parts = after(results[1:], back[2])
    grads = [swap(part, slot) if slot else part for slot, part in enumerate(parts)]
    back[1] = grads[1]
    attended, query_grad = collect(own, back, [both if slot == 1 else 0 for slot in range(slots)])
    grads = after(grads, attended)
    key_grad, value_grad = collect(own, grads, [0] * slots)
    return (attended, query_grad, key_grad, value_grad)


def solution(mesh):
    slots = mesh.shape["ctx"]

    def on_device(query_rows, *others):
        if query_rows.shape[1] == slots >= 4 and slots & (slots - 1) == 0:
            return exchange_plan(slots, query_rows, *others)
        return gather_plan(query_rows, *others)

    rows = P(("groups", "ctx"), ("head", "aux"), None)
    return jax.shard_map(
        on_device,
        mesh=mesh,
        in_specs=(rows, rows, rows, rows, P(("head", "aux"), None), P()),
        out_specs=(rows, rows, rows, rows),
        check_vma=False,
    )
```

```python
import functools
import math

import jax
import jax.numpy as jnp
from jax import lax
from jax.experimental import pallas as pl
from jax.experimental.pallas import tpu as pltpu
from jax.sharding import PartitionSpec as P

FRAME_TOK = 256


def narrowed(values):
    narrow = lax.optimization_barrier(values.astype(jnp.bfloat16))
    return narrow.astype(jnp.float32)


def keep_same(carried):
    return carried


def shard_frames(frame_map, shard_id, frame_count):
    return lax.dynamic_slice_in_dim(frame_map, shard_id * frame_count, frame_count)


def frame_allowed(band_rows, query_frames, key_frames):
    distance = jnp.abs(query_frames[:, None] - key_frames[None, :])
    offsets = jnp.arange(band_rows.shape[1], dtype=jnp.int32)
    matches = (distance[:, :, None] == offsets[None, None, :]).astype(jnp.int32)
    allowed_sum = jnp.sum(matches[None, :, :, :] * band_rows[:, None, None, :], axis=3)
    return allowed_sum > 0


def tile_scores(queries, keys_part, allowed, scaling):
    products = (
        jnp.einsum("qhd,khd->hqk", queries, keys_part, preferred_element_type=jnp.float32) * scaling
    )
    head_count, query_count, key_count = products.shape
    shaped = products.reshape(head_count, allowed.shape[1], FRAME_TOK, allowed.shape[2], FRAME_TOK)
    masked = jnp.where(allowed[:, :, None, :, None], shaped, -jnp.inf)
    return masked.reshape(head_count, query_count, key_count)


def forward_tile(carried, queries, keys_part, values_part, allowed, scaling):
    run_max, run_sum, weighted = carried
    scores = tile_scores(queries, keys_part, allowed, scaling)
    new_max = jnp.maximum(run_max, jnp.max(scores, axis=2))
    weights = jnp.exp(scores - new_max[:, :, None])
    factor = jnp.exp(run_max - new_max)
    run_sum = run_sum * factor + jnp.sum(weights, axis=2)
    update = jnp.einsum(
        "hqk,khd->qhd",
        weights.astype(jnp.bfloat16),
        values_part,
        preferred_element_type=jnp.float32,
    )
    weighted = weighted * factor.T[:, :, None] + update
    return (new_max, run_sum, weighted)


def query_grad_term(
    queries, grad_rows, log_total, row_delta, keys_part, values_part, allowed, scaling
):
    scores = tile_scores(queries, keys_part, allowed, scaling)
    probabilities = jnp.exp(scores - log_total[:, :, None])
    prob_grad = jnp.einsum(
        "qhd,khd->hqk", grad_rows, values_part, preferred_element_type=jnp.float32
    )
    score_grad = (probabilities * (prob_grad - row_delta[:, :, None])).astype(jnp.bfloat16)
    return jnp.einsum("hqk,khd->qhd", score_grad, keys_part, preferred_element_type=jnp.float32)


def key_grad_terms(
    queries, grad_rows, log_total, row_delta, keys_part, values_part, allowed, scaling
):
    scores = tile_scores(queries, keys_part, allowed, scaling)
    probabilities = jnp.exp(scores - log_total[:, :, None])
    value_term = jnp.einsum(
        "hqk,qhd->khd",
        probabilities.astype(jnp.bfloat16),
        grad_rows,
        preferred_element_type=jnp.float32,
    )
    prob_grad = jnp.einsum(
        "qhd,khd->hqk", grad_rows, values_part, preferred_element_type=jnp.float32
    )
    score_grad = (probabilities * (prob_grad - row_delta[:, :, None])).astype(jnp.bfloat16)
    key_term = scaling * jnp.einsum(
        "hqk,qhd->khd", score_grad, queries, preferred_element_type=jnp.float32
    )
    return (key_term, value_term)


def shard_scan(step, carried, pieces, shard_rows):
    shard_total = pieces[0].shape[0] // shard_rows
    stacked = tuple(
        (member.reshape((shard_total, shard_rows) + member.shape[1:]) for member in pieces)
    )
    shard_ids = jnp.arange(shard_total, dtype=jnp.int32)

    def advance(current, element):
        return (step(current, element[1], element[0]), None)

    result, unused_out = lax.scan(advance, carried, (shard_ids, stacked))
    return result


def gather_plan(query_rows, key_rows, value_rows, out_grad, head_band, frame_map):
    shard_rows = query_rows.shape[0]
    head_count = query_rows.shape[1]
    head_width = query_rows.shape[2]
    frame_count = shard_rows // FRAME_TOK
    scaling = head_width ** (-0.5)
    own_index = lax.axis_index("ctx")
    own_frames = shard_frames(frame_map, own_index, frame_count)
    all_keys = lax.all_gather(key_rows, "ctx", axis=0, tiled=True)
    all_values = lax.all_gather(value_rows, "ctx", axis=0, tiled=True)

    def forward_step(carried, pieces, shard_id):
        allowed = frame_allowed(
            head_band, own_frames, shard_frames(frame_map, shard_id, frame_count)
        )

        def forward_compute(current):
            return forward_tile(current, query_rows, pieces[0], pieces[1], allowed, scaling)

        return lax.cond(jnp.any(allowed), forward_compute, keep_same, carried)

    start_state = (
        jnp.full((head_count, shard_rows), -1e30, jnp.float32),
        jnp.zeros((head_count, shard_rows), jnp.float32),
        jnp.zeros((shard_rows, head_count, head_width), jnp.float32),
    )
    forward_state = shard_scan(forward_step, start_state, (all_keys, all_values), shard_rows)
    run_max, run_sum, weighted = forward_state
    out_full = weighted / run_sum.T[:, :, None]
    attended = out_full.astype(jnp.bfloat16)
    log_total = run_max + jnp.log(run_sum)
    row_delta = jnp.sum(out_grad.astype(jnp.float32) * out_full, axis=2).T
    zero_rows = jnp.zeros((shard_rows, head_count, head_width), jnp.float32)

    def backward_step(carried, pieces, shard_id):
        allowed = frame_allowed(
            head_band, own_frames, shard_frames(frame_map, shard_id, frame_count)
        )

        def backward_compute(current):
            return current + query_grad_term(
                query_rows, out_grad, log_total, row_delta, pieces[0], pieces[1], allowed, scaling
            )

        return lax.cond(jnp.any(allowed), backward_compute, keep_same, carried)

    query_sum = shard_scan(backward_step, zero_rows, (all_keys, all_values), shard_rows)
    query_grad = (scaling * query_sum).astype(jnp.bfloat16)
    all_stats = (
        lax.all_gather(log_total, "ctx", axis=1, tiled=True),
        lax.all_gather(row_delta, "ctx", axis=1, tiled=True),
    )

    def key_step(carried, pieces, shard_id):
        allowed = frame_allowed(
            head_band, shard_frames(frame_map, shard_id, frame_count), own_frames
        )
        stat_log = lax.dynamic_slice_in_dim(all_stats[0], shard_id * shard_rows, shard_rows, 1)
        stat_delta = lax.dynamic_slice_in_dim(all_stats[1], shard_id * shard_rows, shard_rows, 1)

        def key_compute(current):
            key_term, value_term = key_grad_terms(
                pieces[0], pieces[1], stat_log, stat_delta, key_rows, value_rows, allowed, scaling
            )
            return (current[0] + narrowed(key_term), current[1] + narrowed(value_term))

        return lax.cond(jnp.any(allowed), key_compute, keep_same, carried)

    key_sum, value_sum = shard_scan(
        key_step,
        (zero_rows, zero_rows),
        (
            lax.all_gather(query_rows, "ctx", axis=0, tiled=True),
            lax.all_gather(out_grad, "ctx", axis=0, tiled=True),
        ),
        shard_rows,
    )
    key_grad = key_sum.astype(jnp.bfloat16)
    value_grad = value_sum.astype(jnp.bfloat16)
    return (attended, query_grad, key_grad, value_grad)


VMEM = pl.BlockSpec(memory_space=pltpu.VMEM)
SMEM = pl.BlockSpec(memory_space=pltpu.SMEM)
HBM = pl.BlockSpec(memory_space=pltpu.HBM)


def spread_body(slots, chunks, own_ref, *refs):
    sources, refs = refs[:4], refs[4:]
    kv_refs, qg_refs, (stage, wide, arrived) = refs[: slots - 1], refs[slots - 1 : -3], refs[-3:]
    rows, width = sources[0].shape
    part_rows = rows // chunks
    part_tokens = part_rows // slots
    own = own_ref[0]
    copies = [
        [
            pltpu.make_async_copy(
                source.at[pl.ds(chunk * part_rows, part_rows), :],
                stage.at[which, pl.ds(chunk * part_rows, part_rows), :],
                arrived.at[which, chunk],
            )
            for chunk in range(chunks)
        ]
        for which, source in enumerate(sources)
    ]
    for array in copies:
        for copy in array:
            copy.start()
    for which, array in enumerate(copies):
        for chunk, copy in enumerate(array):
            copy.wait()
            first = chunk * part_rows
            wide[which, first : first + part_rows, :] = stage[
                which, first : first + part_rows, :
            ].astype(jnp.float32)
            tokens = slice(chunk * part_tokens, (chunk + 1) * part_tokens)
            for slot in range(slots):
                picked = wide[which, pl.ds(first + (own ^ slot), part_tokens, stride=slots), :]
                column = (which % 2) * width
                if which < 2 and slot == 1:
                    target, column = qg_refs[1], column + 2 * width
                elif which < 2:
                    target = kv_refs[max(slot - 1, 0)]
                else:
                    target = qg_refs[slot]
                target[tokens, column : column + width] = picked.astype(jnp.bfloat16)


def spread(own, keys, values, queries, grads, chunks=4):
    tokens, slots, width = keys.shape
    rows = tokens * slots
    pair = jax.ShapeDtypeStruct((tokens, 2 * width), jnp.bfloat16)
    both = jax.ShapeDtypeStruct((tokens, 4 * width), jnp.bfloat16)
    results = pl.pallas_call(
        functools.partial(spread_body, slots, chunks),
        out_shape=[pair] * (slots - 1) + [pair, both] + [pair] * (slots - 2),
        in_specs=[SMEM] + [HBM] * 4,
        out_specs=[VMEM] * (2 * slots - 1),
        scratch_shapes=[
            pltpu.VMEM((4, rows, width), jnp.bfloat16),
            pltpu.VMEM((4, rows, width), jnp.float32),
            pltpu.SemaphoreType.DMA((4, chunks)),
        ],
        cost_estimate=pl.CostEstimate(flops=0, transcendentals=0, bytes_accessed=16 * rows * width),
        compiler_params=pltpu.CompilerParams(vmem_limit_bytes=16 << 20),
        name="spread",
    )(
        own,
        *(
            pltpu.with_memory_space_constraint(array.reshape(rows, width), pltpu.HBM)
            for array in (keys, values, queries, grads)
        ),
    )
    kv, qg = list(results[: slots - 1]), list(results[slots - 1 :])
    return [kv[0], None] + kv[1:], qg


def collect_body(slots, starts, own_ref, *rest):
    pieces, (first_ref, second_ref, wide) = rest[:slots], rest[slots:]
    width = first_ref.shape[1]
    tokens = first_ref.shape[0] // slots
    own = own_ref[0]
    for part, target in enumerate((first_ref, second_ref)):
        for slot in range(slots):
            start = starts[slot] + part * width
            piece = pieces[slot][:, start : start + width]
            wide[pl.ds(own ^ slot, tokens, stride=slots), :] = piece.astype(jnp.float32)
        target[...] = wide[...].astype(jnp.bfloat16)


def collect(own, pieces, starts):
    slots = len(pieces)
    tokens, width = pieces[0].shape[0], pieces[0].shape[1] // 2
    rows = tokens * slots
    first, second = pl.pallas_call(
        functools.partial(collect_body, slots, starts),
        out_shape=[jax.ShapeDtypeStruct((rows, width), jnp.bfloat16)] * 2,
        in_specs=[SMEM] + [VMEM] * slots,
        out_specs=[VMEM] * 2,
        scratch_shapes=[pltpu.VMEM((rows, width), jnp.float32)],
        cost_estimate=pl.CostEstimate(flops=0, transcendentals=0, bytes_accessed=8 * rows * width),
        compiler_params=pltpu.CompilerParams(vmem_limit_bytes=12 << 20),
        name="collect",
    )(own, *pieces)
    return first.reshape(tokens, slots, width), second.reshape(tokens, slots, width)


def join_body(slots, *refs):
    pieces, (rows_ref, flat_ref) = refs[:slots], refs[slots:]
    tokens = pieces[0].shape[0]
    both = rows_ref.shape[1]
    for slot in range(slots):
        piece = pieces[slot][:, pieces[slot].shape[1] - both :]
        rows_ref[slot * tokens : (slot + 1) * tokens, :] = piece
        flat_ref[:, slot * tokens : (slot + 1) * tokens] = piece.T


def join(pieces):
    slots = len(pieces)
    tokens, both = pieces[0].shape
    return pl.pallas_call(
        functools.partial(join_body, slots),
        out_shape=[
            jax.ShapeDtypeStruct((slots * tokens, both), jnp.bfloat16),
            jax.ShapeDtypeStruct((both, slots * tokens), jnp.bfloat16),
        ],
        in_specs=[VMEM] * slots,
        out_specs=[VMEM] * 2,
        cost_estimate=pl.CostEstimate(
            flops=0, transcendentals=0, bytes_accessed=6 * slots * tokens * both
        ),
        compiler_params=pltpu.CompilerParams(vmem_limit_bytes=12 << 20),
        name="join",
    )(*pieces)


def attend_body(
    slots, slot, first, last, own_ref, band_ref, map_ref, qg_ref, kv_ref, kvt_ref, *rest
):
    if first:
        sums_in = None
    else:
        sums_in, rest = rest[0], rest[1:]
    if last:
        passenger, rest = rest[0], rest[1:]
    out_ref, rest = rest[0], rest[1:]
    if last:
        parts, rest = rest[:slots], rest[slots:]
        sums_ref, rest = rest[0], rest[1:]
        parts[1][:, kv_ref.shape[1] :] = passenger[...]
    else:
        sums_ref, rest = rest[0], rest[1:]
    scores_ref, out_acc, grad_acc = rest
    tokens = qg_ref.shape[0]
    width = kv_ref.shape[1] // 2
    frames = tokens // FRAME_TOK
    keys = kv_ref.shape[0]
    scaling = width ** (-0.5)
    power = scaling * math.log2(math.e)
    own = own_ref[0]

    queries = qg_ref[:, :width]
    grads = qg_ref[:, width : 2 * width]
    queries_t = queries.T
    grads_t = grads.T
    lane = lax.broadcasted_iota(jnp.int32, (1, tokens), 1)

    def allowed_row(tile):
        key_frame = map_ref[(own ^ (tile // frames)) * frames + tile % frames]
        row = jnp.zeros((1, tokens), jnp.int32)
        for frame in range(frames):
            gap = jnp.abs(map_ref[(own ^ slot) * frames + frame] - key_frame)
            row = jnp.where(lane // FRAME_TOK == frame, band_ref[own, gap], row)
        return row == 1

    def tile_rows(tile):
        return pl.ds(pl.multiple_of(tile * FRAME_TOK, FRAME_TOK), FRAME_TOK)

    def score_step(tile, row_max):
        rows = tile_rows(tile)
        scores = jnp.dot(kv_ref[rows, :width], queries_t, preferred_element_type=jnp.float32)
        scores_ref[rows, :] = scores
        tile_max = jnp.max(scores, axis=0, keepdims=True)
        return jnp.maximum(row_max, jnp.where(allowed_row(tile), tile_max, -jnp.inf))

    tiles = keys // FRAME_TOK
    row_max = lax.fori_loop(0, tiles, score_step, jnp.full((1, tokens), -jnp.inf, jnp.float32), unroll=8)
    row_max = row_max * power
    out_acc[...] = jnp.zeros_like(out_acc)

    def weight_step(tile, total):
        rows = tile_rows(tile)
        shift = jnp.where(allowed_row(tile), row_max, jnp.inf)
        weights = jnp.exp2(scores_ref[rows, :] * power - shift)
        scores_ref[rows, :] = weights
        out_acc[...] += jnp.dot(
            kvt_ref[width:, rows], weights.astype(jnp.bfloat16), preferred_element_type=jnp.float32
        )
        return total + jnp.sum(weights, axis=0, keepdims=True)

    total = lax.fori_loop(0, tiles, weight_step, jnp.zeros((1, tokens), jnp.float32), unroll=8)
    inverse = 1.0 / total
    out_full = out_acc[...] * inverse
    delta = jnp.sum(out_full * grads_t.astype(jnp.float32), axis=0, keepdims=True)
    out_ref[:, :width] = out_full.T.astype(jnp.bfloat16)
    grad_acc[...] = jnp.zeros_like(grad_acc)

    def grad_step(tile, carried):
        rows = tile_rows(tile)
        probabilities = scores_ref[rows, :] * inverse
        prob_grad = jnp.dot(kv_ref[rows, width:], grads_t, preferred_element_type=jnp.float32)
        score_grad = (probabilities * (prob_grad - delta)).astype(jnp.bfloat16)
        value_term = jnp.dot(
            probabilities.astype(jnp.bfloat16), grads, preferred_element_type=jnp.float32
        )
        key_term = jnp.dot(score_grad, queries, preferred_element_type=jnp.float32)
        grad_acc[...] += jnp.dot(
            kvt_ref[:width, rows], score_grad, preferred_element_type=jnp.float32
        )
        if first:
            sums_ref[rows, :width] = key_term
            sums_ref[rows, width:] = value_term
        else:
            sums_ref[rows, :width] = sums_in[rows, :width] + key_term
            sums_ref[rows, width:] = sums_in[rows, width:] + value_term
        return carried

    lax.fori_loop(0, tiles, grad_step, 0, unroll=8)
    out_ref[:, width:] = (grad_acc[...] * scaling).T.astype(jnp.bfloat16)
    if last:
        for part in range(slots):
            rows = slice(part * tokens, (part + 1) * tokens)
            parts[part][:, :width] = (sums_ref[rows, :width] * scaling).astype(jnp.bfloat16)
            parts[part][:, width : 2 * width] = sums_ref[rows, width:].astype(jnp.bfloat16)


def attend(slots, slot, first, last, own, head_band, frame_map, pair, kv, kvt, sums, passenger=None):
    tokens, both = pair.shape[0], kv.shape[1]
    keys, width = kv.shape[0], both // 2
    piece = jax.ShapeDtypeStruct((tokens, both), jnp.bfloat16)
    sums_shape = jax.ShapeDtypeStruct((keys, both), jnp.float32)
    outs = [piece] + ([piece] * slots if last else [sums_shape])
    if last:
        outs[2] = jax.ShapeDtypeStruct((tokens, 2 * both), jnp.bfloat16)
    scratch = [
        pltpu.VMEM((keys, tokens), jnp.float32),
        pltpu.VMEM((width, tokens), jnp.float32),
        pltpu.VMEM((width, tokens), jnp.float32),
    ]
    if last:
        scratch = [pltpu.VMEM((keys, both), jnp.float32)] + scratch
    operands = [own, head_band, frame_map, pair, kv, kvt] + ([] if first else [sums])
    if last:
        operands.append(passenger)
    return pl.pallas_call(
        functools.partial(attend_body, slots, slot, first, last),
        out_shape=outs,
        in_specs=[SMEM] * 3 + [VMEM] * (len(operands) - 3),
        out_specs=[VMEM] * len(outs),
        scratch_shapes=scratch,
        input_output_aliases={} if first or last else {6: 1},
        cost_estimate=pl.CostEstimate(
            flops=12 * tokens * keys * width,
            transcendentals=tokens * keys,
            bytes_accessed=10 * keys * both,
        ),
        compiler_params=pltpu.CompilerParams(vmem_limit_bytes=24 << 20),
        name="attend",
    )(*operands)


def exchange_plan(slots, query_rows, key_rows, value_rows, out_grad, head_band, frame_map):
    own_index = lax.axis_index("ctx").astype(jnp.int32)
    own = own_index.reshape(1)

    def swap(piece, slot):
        return lax.ppermute(piece, "ctx", [(place, place ^ slot) for place in range(slots)])

    def after(values, *gates):
        return lax.optimization_barrier((values, gates))[0]

    kv_slots, qg_slots = spread(own, key_rows, value_rows, query_rows, out_grad)
    for slot in range(2, slots):
        kv_slots[slot] = swap(kv_slots[slot], slot)
    kv_slots[1] = qg_slots[1] = swap(qg_slots[1], 1)
    kv, kvt = join(kv_slots)
    both = kv.shape[1]
    back = list(kv_slots)
    gate = kv_slots[2]
    sums = None
    for slot in range(slots):
        last = slot == slots - 1
        if slot + 2 < slots:
            qg_slots[slot + 2] = swap(after(qg_slots[slot + 2], gate), slot + 2)
        results = attend(
            slots, slot, slot == 0, last, own, head_band, frame_map, qg_slots[slot], kv, kvt, sums,
            back[1],
        )
        back[slot] = results[0] if slot < 2 else swap(results[0], slot)
        sums = results[1]
        gate = results[0]
    grads = list(results[1:])
    grads[2:] = after(grads[2:], back[2])
    grads = [swap(part, slot) if slot else part for slot, part in enumerate(grads)]
    back[1] = grads[1]
    attended, query_grad = collect(own, back, [both if slot == 1 else 0 for slot in range(slots)])
    grads = after(grads, attended)
    key_grad, value_grad = collect(own, grads, [0] * slots)
    return (attended, query_grad, key_grad, value_grad)


def solution(mesh):
    slots = mesh.shape["ctx"]

    def on_device(query_rows, *others):
        if query_rows.shape[1] == slots >= 4 and slots & (slots - 1) == 0:
            return exchange_plan(slots, query_rows, *others)
        return gather_plan(query_rows, *others)

    rows = P(("groups", "ctx"), ("head", "aux"), None)
    return jax.shard_map(
        on_device,
        mesh=mesh,
        in_specs=(rows, rows, rows, rows, P(("head", "aux"), None), P()),
        out_specs=(rows, rows, rows, rows),
        check_vma=False,
    )
```

```python
import functools
import math

import jax
import jax.numpy as jnp
from jax import lax
from jax.experimental import pallas as pl
from jax.experimental.pallas import tpu as pltpu
from jax.sharding import PartitionSpec as P

FRAME_TOK = 256


def narrowed(values):
    narrow = lax.optimization_barrier(values.astype(jnp.bfloat16))
    return narrow.astype(jnp.float32)


def keep_same(carried):
    return carried


def shard_frames(frame_map, shard_id, frame_count):
    return lax.dynamic_slice_in_dim(frame_map, shard_id * frame_count, frame_count)


def frame_allowed(band_rows, query_frames, key_frames):
    distance = jnp.abs(query_frames[:, None] - key_frames[None, :])
    offsets = jnp.arange(band_rows.shape[1], dtype=jnp.int32)
    matches = (distance[:, :, None] == offsets[None, None, :]).astype(jnp.int32)
    allowed_sum = jnp.sum(matches[None, :, :, :] * band_rows[:, None, None, :], axis=3)
    return allowed_sum > 0


def tile_scores(queries, keys_part, allowed, scaling):
    products = (
        jnp.einsum("qhd,khd->hqk", queries, keys_part, preferred_element_type=jnp.float32) * scaling
    )
    head_count, query_count, key_count = products.shape
    shaped = products.reshape(head_count, allowed.shape[1], FRAME_TOK, allowed.shape[2], FRAME_TOK)
    masked = jnp.where(allowed[:, :, None, :, None], shaped, -jnp.inf)
    return masked.reshape(head_count, query_count, key_count)


def forward_tile(carried, queries, keys_part, values_part, allowed, scaling):
    run_max, run_sum, weighted = carried
    scores = tile_scores(queries, keys_part, allowed, scaling)
    new_max = jnp.maximum(run_max, jnp.max(scores, axis=2))
    weights = jnp.exp(scores - new_max[:, :, None])
    factor = jnp.exp(run_max - new_max)
    run_sum = run_sum * factor + jnp.sum(weights, axis=2)
    update = jnp.einsum(
        "hqk,khd->qhd",
        weights.astype(jnp.bfloat16),
        values_part,
        preferred_element_type=jnp.float32,
    )
    weighted = weighted * factor.T[:, :, None] + update
    return (new_max, run_sum, weighted)


def query_grad_term(
    queries, grad_rows, log_total, row_delta, keys_part, values_part, allowed, scaling
):
    scores = tile_scores(queries, keys_part, allowed, scaling)
    probabilities = jnp.exp(scores - log_total[:, :, None])
    prob_grad = jnp.einsum(
        "qhd,khd->hqk", grad_rows, values_part, preferred_element_type=jnp.float32
    )
    score_grad = (probabilities * (prob_grad - row_delta[:, :, None])).astype(jnp.bfloat16)
    return jnp.einsum("hqk,khd->qhd", score_grad, keys_part, preferred_element_type=jnp.float32)


def key_grad_terms(
    queries, grad_rows, log_total, row_delta, keys_part, values_part, allowed, scaling
):
    scores = tile_scores(queries, keys_part, allowed, scaling)
    probabilities = jnp.exp(scores - log_total[:, :, None])
    value_term = jnp.einsum(
        "hqk,qhd->khd",
        probabilities.astype(jnp.bfloat16),
        grad_rows,
        preferred_element_type=jnp.float32,
    )
    prob_grad = jnp.einsum(
        "qhd,khd->hqk", grad_rows, values_part, preferred_element_type=jnp.float32
    )
    score_grad = (probabilities * (prob_grad - row_delta[:, :, None])).astype(jnp.bfloat16)
    key_term = scaling * jnp.einsum(
        "hqk,qhd->khd", score_grad, queries, preferred_element_type=jnp.float32
    )
    return (key_term, value_term)


def shard_scan(step, carried, pieces, shard_rows):
    shard_total = pieces[0].shape[0] // shard_rows
    stacked = tuple(
        (member.reshape((shard_total, shard_rows) + member.shape[1:]) for member in pieces)
    )
    shard_ids = jnp.arange(shard_total, dtype=jnp.int32)

    def advance(current, element):
        return (step(current, element[1], element[0]), None)

    result, unused_out = lax.scan(advance, carried, (shard_ids, stacked))
    return result


def gather_plan(query_rows, key_rows, value_rows, out_grad, head_band, frame_map):
    shard_rows = query_rows.shape[0]
    head_count = query_rows.shape[1]
    head_width = query_rows.shape[2]
    frame_count = shard_rows // FRAME_TOK
    scaling = head_width ** (-0.5)
    own_index = lax.axis_index("ctx")
    own_frames = shard_frames(frame_map, own_index, frame_count)
    all_keys = lax.all_gather(key_rows, "ctx", axis=0, tiled=True)
    all_values = lax.all_gather(value_rows, "ctx", axis=0, tiled=True)

    def forward_step(carried, pieces, shard_id):
        allowed = frame_allowed(
            head_band, own_frames, shard_frames(frame_map, shard_id, frame_count)
        )

        def forward_compute(current):
            return forward_tile(current, query_rows, pieces[0], pieces[1], allowed, scaling)

        return lax.cond(jnp.any(allowed), forward_compute, keep_same, carried)

    start_state = (
        jnp.full((head_count, shard_rows), -1e30, jnp.float32),
        jnp.zeros((head_count, shard_rows), jnp.float32),
        jnp.zeros((shard_rows, head_count, head_width), jnp.float32),
    )
    forward_state = shard_scan(forward_step, start_state, (all_keys, all_values), shard_rows)
    run_max, run_sum, weighted = forward_state
    out_full = weighted / run_sum.T[:, :, None]
    attended = out_full.astype(jnp.bfloat16)
    log_total = run_max + jnp.log(run_sum)
    row_delta = jnp.sum(out_grad.astype(jnp.float32) * out_full, axis=2).T
    zero_rows = jnp.zeros((shard_rows, head_count, head_width), jnp.float32)

    def backward_step(carried, pieces, shard_id):
        allowed = frame_allowed(
            head_band, own_frames, shard_frames(frame_map, shard_id, frame_count)
        )

        def backward_compute(current):
            return current + query_grad_term(
                query_rows, out_grad, log_total, row_delta, pieces[0], pieces[1], allowed, scaling
            )

        return lax.cond(jnp.any(allowed), backward_compute, keep_same, carried)

    query_sum = shard_scan(backward_step, zero_rows, (all_keys, all_values), shard_rows)
    query_grad = (scaling * query_sum).astype(jnp.bfloat16)
    all_stats = (
        lax.all_gather(log_total, "ctx", axis=1, tiled=True),
        lax.all_gather(row_delta, "ctx", axis=1, tiled=True),
    )

    def key_step(carried, pieces, shard_id):
        allowed = frame_allowed(
            head_band, shard_frames(frame_map, shard_id, frame_count), own_frames
        )
        stat_log = lax.dynamic_slice_in_dim(all_stats[0], shard_id * shard_rows, shard_rows, 1)
        stat_delta = lax.dynamic_slice_in_dim(all_stats[1], shard_id * shard_rows, shard_rows, 1)

        def key_compute(current):
            key_term, value_term = key_grad_terms(
                pieces[0], pieces[1], stat_log, stat_delta, key_rows, value_rows, allowed, scaling
            )
            return (current[0] + narrowed(key_term), current[1] + narrowed(value_term))

        return lax.cond(jnp.any(allowed), key_compute, keep_same, carried)

    key_sum, value_sum = shard_scan(
        key_step,
        (zero_rows, zero_rows),
        (
            lax.all_gather(query_rows, "ctx", axis=0, tiled=True),
            lax.all_gather(out_grad, "ctx", axis=0, tiled=True),
        ),
        shard_rows,
    )
    key_grad = key_sum.astype(jnp.bfloat16)
    value_grad = value_sum.astype(jnp.bfloat16)
    return (attended, query_grad, key_grad, value_grad)


VMEM = pl.BlockSpec(memory_space=pltpu.VMEM)
SMEM = pl.BlockSpec(memory_space=pltpu.SMEM)
HBM = pl.BlockSpec(memory_space=pltpu.HBM)


def spread_body(slots, chunks, carried, own_ref, *refs):
    sources, refs = refs[:2], refs[2:]
    passenger, refs = (refs[0], refs[1:]) if carried else (None, refs)
    outs, (stage, wide, arrived) = refs[:slots], refs[slots:]
    rows, width = sources[0].shape
    part_rows = rows // chunks
    part_tokens = part_rows // slots
    own = own_ref[0]
    copies = [
        pltpu.make_async_copy(
            source.at[pl.ds(chunk * part_rows, part_rows), :],
            stage.at[which, pl.ds(chunk * part_rows, part_rows), :],
            arrived.at[which, chunk],
        )
        for which, source in enumerate(sources)
        for chunk in range(chunks)
    ]
    for copy in copies:
        copy.start()
    if carried:
        outs[1][:, 2 * width :] = passenger[...]
    for step, copy in enumerate(copies):
        which, chunk = divmod(step, chunks)
        first = chunk * part_rows
        copy.wait()
        wide[which, first : first + part_rows, :] = stage[
            which, first : first + part_rows, :
        ].astype(jnp.float32)
        tokens = slice(chunk * part_tokens, (chunk + 1) * part_tokens)
        for slot in range(slots):
            picked = wide[which, pl.ds(first + (own ^ slot), part_tokens, stride=slots), :]
            outs[slot][tokens, which * width : (which + 1) * width] = picked.astype(jnp.bfloat16)


def spread(own, first, second, passenger=None, chunks=4):
    tokens, slots, width = first.shape
    rows = tokens * slots
    shapes = [jax.ShapeDtypeStruct((tokens, 2 * width), jnp.bfloat16)] * slots
    operands = [own] + [
        pltpu.with_memory_space_constraint(array.reshape(rows, width), pltpu.HBM)
        for array in (first, second)
    ]
    specs = [SMEM, HBM, HBM]
    if passenger is not None:
        operands.append(passenger)
        specs.append(VMEM)
        shapes[1] = jax.ShapeDtypeStruct((tokens, 4 * width), jnp.bfloat16)
    return list(
        pl.pallas_call(
            functools.partial(spread_body, slots, chunks, passenger is not None),
            out_shape=shapes,
            in_specs=specs,
            out_specs=[VMEM] * slots,
            scratch_shapes=[
                pltpu.VMEM((2, rows, width), jnp.bfloat16),
                pltpu.VMEM((2, rows, width), jnp.float32),
                pltpu.SemaphoreType.DMA((2, chunks)),
            ],
            cost_estimate=pl.CostEstimate(
                flops=0, transcendentals=0, bytes_accessed=8 * rows * width
            ),
            compiler_params=pltpu.CompilerParams(vmem_limit_bytes=12 << 20),
            name="spread",
        )(*operands)
    )


def collect_body(slots, starts, own_ref, *rest):
    pieces, (first_ref, second_ref, wide) = rest[:slots], rest[slots:]
    width = first_ref.shape[1]
    tokens = first_ref.shape[0] // slots
    own = own_ref[0]
    for part, target in enumerate((first_ref, second_ref)):
        for slot in range(slots):
            start = starts[slot] + part * width
            piece = pieces[slot][:, start : start + width]
            wide[pl.ds(own ^ slot, tokens, stride=slots), :] = piece.astype(jnp.float32)
        target[...] = wide[...].astype(jnp.bfloat16)


def collect(own, pieces, starts):
    slots = len(pieces)
    tokens, width = pieces[0].shape[0], pieces[0].shape[1] // 2
    rows = tokens * slots
    first, second = pl.pallas_call(
        functools.partial(collect_body, slots, starts),
        out_shape=[jax.ShapeDtypeStruct((rows, width), jnp.bfloat16)] * 2,
        in_specs=[SMEM] + [VMEM] * slots,
        out_specs=[VMEM] * 2,
        scratch_shapes=[pltpu.VMEM((rows, width), jnp.float32)],
        cost_estimate=pl.CostEstimate(flops=0, transcendentals=0, bytes_accessed=8 * rows * width),
        compiler_params=pltpu.CompilerParams(vmem_limit_bytes=12 << 20),
        name="collect",
    )(own, *pieces)
    return first.reshape(tokens, slots, width), second.reshape(tokens, slots, width)


def join_body(slots, *refs):
    pieces, (rows_ref, flat_ref) = refs[:slots], refs[slots:]
    tokens = pieces[0].shape[0]
    both = rows_ref.shape[1]
    for slot in range(slots):
        piece = pieces[slot][:, pieces[slot].shape[1] - both :]
        rows_ref[slot * tokens : (slot + 1) * tokens, :] = piece
        flat_ref[:, slot * tokens : (slot + 1) * tokens] = piece.T


def join(pieces):
    slots = len(pieces)
    tokens, both = pieces[0].shape
    return pl.pallas_call(
        functools.partial(join_body, slots),
        out_shape=[
            jax.ShapeDtypeStruct((slots * tokens, both), jnp.bfloat16),
            jax.ShapeDtypeStruct((both, slots * tokens), jnp.bfloat16),
        ],
        in_specs=[VMEM] * slots,
        out_specs=[VMEM] * 2,
        cost_estimate=pl.CostEstimate(
            flops=0, transcendentals=0, bytes_accessed=6 * slots * tokens * both
        ),
        compiler_params=pltpu.CompilerParams(vmem_limit_bytes=12 << 20),
        name="join",
    )(*pieces)


def attend_body(
    slots, slot, first, last, own_ref, band_ref, map_ref, qg_ref, kv_ref, kvt_ref, *rest
):
    if first:
        sums_in = None
    else:
        sums_in, rest = rest[0], rest[1:]
    if last:
        passenger, rest = rest[0], rest[1:]
    out_ref, rest = rest[0], rest[1:]
    if last:
        parts, rest = rest[:slots], rest[slots:]
        sums_ref, rest = rest[0], rest[1:]
        parts[1][:, kv_ref.shape[1] :] = passenger[...]
    else:
        sums_ref, rest = rest[0], rest[1:]
    scores_ref, out_acc, grad_acc = rest
    tokens = qg_ref.shape[0]
    width = kv_ref.shape[1] // 2
    frames = tokens // FRAME_TOK
    keys = kv_ref.shape[0]
    scaling = width ** (-0.5)
    power = scaling * math.log2(math.e)
    own = own_ref[0]

    queries = qg_ref[:, :width]
    grads = qg_ref[:, width : 2 * width]
    queries_t = queries.T
    grads_t = grads.T
    lane = lax.broadcasted_iota(jnp.int32, (1, tokens), 1)

    def allowed_row(tile):
        key_frame = map_ref[(own ^ (tile // frames)) * frames + tile % frames]
        row = jnp.zeros((1, tokens), jnp.int32)
        for frame in range(frames):
            gap = jnp.abs(map_ref[(own ^ slot) * frames + frame] - key_frame)
            row = jnp.where(lane // FRAME_TOK == frame, band_ref[own, gap], row)
        return row == 1

    def tile_rows(tile):
        return pl.ds(pl.multiple_of(tile * FRAME_TOK, FRAME_TOK), FRAME_TOK)

    def score_step(tile, row_max):
        rows = tile_rows(tile)
        scores = jnp.dot(kv_ref[rows, :width], queries_t, preferred_element_type=jnp.float32)
        scores_ref[rows, :] = scores
        tile_max = jnp.max(scores, axis=0, keepdims=True)
        return jnp.maximum(row_max, jnp.where(allowed_row(tile), tile_max, -jnp.inf))

    tiles = keys // FRAME_TOK
    row_max = lax.fori_loop(0, tiles, score_step, jnp.full((1, tokens), -jnp.inf, jnp.float32), unroll=8)
    row_max = row_max * power
    out_acc[...] = jnp.zeros_like(out_acc)

    def weight_step(tile, total):
        rows = tile_rows(tile)
        shift = jnp.where(allowed_row(tile), row_max, jnp.inf)
        weights = jnp.exp2(scores_ref[rows, :] * power - shift)
        scores_ref[rows, :] = weights
        out_acc[...] += jnp.dot(
            kvt_ref[width:, rows], weights.astype(jnp.bfloat16), preferred_element_type=jnp.float32
        )
        return total + jnp.sum(weights, axis=0, keepdims=True)

    total = lax.fori_loop(0, tiles, weight_step, jnp.zeros((1, tokens), jnp.float32), unroll=8)
    inverse = 1.0 / total
    out_full = out_acc[...] * inverse
    delta = jnp.sum(out_full * grads_t.astype(jnp.float32), axis=0, keepdims=True)
    out_ref[:, :width] = out_full.T.astype(jnp.bfloat16)
    grad_acc[...] = jnp.zeros_like(grad_acc)

    def grad_step(tile, carried):
        rows = tile_rows(tile)
        probabilities = scores_ref[rows, :] * inverse
        prob_grad = jnp.dot(kv_ref[rows, width:], grads_t, preferred_element_type=jnp.float32)
        score_grad = (probabilities * (prob_grad - delta)).astype(jnp.bfloat16)
        value_term = jnp.dot(
            probabilities.astype(jnp.bfloat16), grads, preferred_element_type=jnp.float32
        )
        key_term = jnp.dot(score_grad, queries, preferred_element_type=jnp.float32)
        grad_acc[...] += jnp.dot(
            kvt_ref[:width, rows], score_grad, preferred_element_type=jnp.float32
        )
        if first:
            sums_ref[rows, :width] = key_term
            sums_ref[rows, width:] = value_term
        else:
            sums_ref[rows, :width] = sums_in[rows, :width] + key_term
            sums_ref[rows, width:] = sums_in[rows, width:] + value_term
        return carried

    lax.fori_loop(0, tiles, grad_step, 0, unroll=8)
    out_ref[:, width:] = (grad_acc[...] * scaling).T.astype(jnp.bfloat16)
    if last:
        for part in range(slots):
            rows = slice(part * tokens, (part + 1) * tokens)
            parts[part][:, :width] = (sums_ref[rows, :width] * scaling).astype(jnp.bfloat16)
            parts[part][:, width : 2 * width] = sums_ref[rows, width:].astype(jnp.bfloat16)


def attend(slots, slot, first, last, own, head_band, frame_map, pair, kv, kvt, sums, passenger=None):
    tokens, both = pair.shape[0], kv.shape[1]
    keys, width = kv.shape[0], both // 2
    piece = jax.ShapeDtypeStruct((tokens, both), jnp.bfloat16)
    sums_shape = jax.ShapeDtypeStruct((keys, both), jnp.float32)
    outs = [piece] + ([piece] * slots if last else [sums_shape])
    if last:
        outs[2] = jax.ShapeDtypeStruct((tokens, 2 * both), jnp.bfloat16)
    scratch = [
        pltpu.VMEM((keys, tokens), jnp.float32),
        pltpu.VMEM((width, tokens), jnp.float32),
        pltpu.VMEM((width, tokens), jnp.float32),
    ]
    if last:
        scratch = [pltpu.VMEM((keys, both), jnp.float32)] + scratch
    operands = [own, head_band, frame_map, pair, kv, kvt] + ([] if first else [sums])
    if last:
        operands.append(passenger)
    return pl.pallas_call(
        functools.partial(attend_body, slots, slot, first, last),
        out_shape=outs,
        in_specs=[SMEM] * 3 + [VMEM] * (len(operands) - 3),
        out_specs=[VMEM] * len(outs),
        scratch_shapes=scratch,
        input_output_aliases={} if first or last else {6: 1},
        cost_estimate=pl.CostEstimate(
            flops=12 * tokens * keys * width,
            transcendentals=tokens * keys,
            bytes_accessed=10 * keys * both,
        ),
        compiler_params=pltpu.CompilerParams(vmem_limit_bytes=24 << 20),
        name="attend",
    )(*operands)


def exchange_plan(slots, query_rows, key_rows, value_rows, out_grad, head_band, frame_map):
    own_index = lax.axis_index("ctx").astype(jnp.int32)
    own = own_index.reshape(1)

    def swap(piece, slot):
        return lax.ppermute(piece, "ctx", [(place, place ^ slot) for place in range(slots)])

    def after(values, *gates):
        return lax.optimization_barrier((values, gates))[0]

    kv_slots = spread(own, key_rows, value_rows)
    qg_slots = spread(own, query_rows, out_grad)
    for slot in range(1, slots):
        kv_slots[slot] = swap(kv_slots[slot], slot)
    qg_slots[1] = swap(qg_slots[1], 1)
    kv, kvt = join(kv_slots)
    both = kv.shape[1]
    back = list(kv_slots)
    gate = kv_slots[2]
    sums = None
    for slot in range(slots):
        last = slot == slots - 1
        if slot + 2 < slots:
            qg_slots[slot + 2] = swap(after(qg_slots[slot + 2], gate), slot + 2)
        results = attend(
            slots, slot, slot == 0, last, own, head_band, frame_map, qg_slots[slot], kv, kvt, sums,
            back[1],
        )
        back[slot] = results[0] if slot < 2 else swap(results[0], slot)
        sums = results[1]
        gate = results[0]
    grads = list(results[1:])
    grads[2:] = after(grads[2:], back[2])
    grads = [swap(part, slot) if slot else part for slot, part in enumerate(grads)]
    back[1] = grads[1]
    attended, query_grad = collect(own, back, [both if slot == 1 else 0 for slot in range(slots)])
    grads = after(grads, attended)
    key_grad, value_grad = collect(own, grads, [0] * slots)
    return (attended, query_grad, key_grad, value_grad)


def solution(mesh):
    slots = mesh.shape["ctx"]

    def on_device(query_rows, *others):
        if query_rows.shape[1] == slots >= 4 and slots & (slots - 1) == 0:
            return exchange_plan(slots, query_rows, *others)
        return gather_plan(query_rows, *others)

    rows = P(("groups", "ctx"), ("head", "aux"), None)
    return jax.shard_map(
        on_device,
        mesh=mesh,
        in_specs=(rows, rows, rows, rows, P(("head", "aux"), None), P()),
        out_specs=(rows, rows, rows, rows),
        check_vma=False,
    )
```

```python
import functools
import math

import jax
import jax.numpy as jnp
from jax import lax
from jax.experimental import pallas as pl
from jax.experimental.pallas import tpu as pltpu
from jax.sharding import PartitionSpec as P

FRAME_TOK = 256


def narrowed(values):
    narrow = lax.optimization_barrier(values.astype(jnp.bfloat16))
    return narrow.astype(jnp.float32)


def keep_same(carried):
    return carried


def shard_frames(frame_map, shard_id, frame_count):
    return lax.dynamic_slice_in_dim(frame_map, shard_id * frame_count, frame_count)


def frame_allowed(band_rows, query_frames, key_frames):
    distance = jnp.abs(query_frames[:, None] - key_frames[None, :])
    offsets = jnp.arange(band_rows.shape[1], dtype=jnp.int32)
    matches = (distance[:, :, None] == offsets[None, None, :]).astype(jnp.int32)
    allowed_sum = jnp.sum(matches[None, :, :, :] * band_rows[:, None, None, :], axis=3)
    return allowed_sum > 0


def tile_scores(queries, keys_part, allowed, scaling):
    products = (
        jnp.einsum("qhd,khd->hqk", queries, keys_part, preferred_element_type=jnp.float32) * scaling
    )
    head_count, query_count, key_count = products.shape
    shaped = products.reshape(head_count, allowed.shape[1], FRAME_TOK, allowed.shape[2], FRAME_TOK)
    masked = jnp.where(allowed[:, :, None, :, None], shaped, -jnp.inf)
    return masked.reshape(head_count, query_count, key_count)


def forward_tile(carried, queries, keys_part, values_part, allowed, scaling):
    run_max, run_sum, weighted = carried
    scores = tile_scores(queries, keys_part, allowed, scaling)
    new_max = jnp.maximum(run_max, jnp.max(scores, axis=2))
    weights = jnp.exp(scores - new_max[:, :, None])
    factor = jnp.exp(run_max - new_max)
    run_sum = run_sum * factor + jnp.sum(weights, axis=2)
    update = jnp.einsum(
        "hqk,khd->qhd",
        weights.astype(jnp.bfloat16),
        values_part,
        preferred_element_type=jnp.float32,
    )
    weighted = weighted * factor.T[:, :, None] + update
    return (new_max, run_sum, weighted)


def query_grad_term(
    queries, grad_rows, log_total, row_delta, keys_part, values_part, allowed, scaling
):
    scores = tile_scores(queries, keys_part, allowed, scaling)
    probabilities = jnp.exp(scores - log_total[:, :, None])
    prob_grad = jnp.einsum(
        "qhd,khd->hqk", grad_rows, values_part, preferred_element_type=jnp.float32
    )
    score_grad = (probabilities * (prob_grad - row_delta[:, :, None])).astype(jnp.bfloat16)
    return jnp.einsum("hqk,khd->qhd", score_grad, keys_part, preferred_element_type=jnp.float32)


def key_grad_terms(
    queries, grad_rows, log_total, row_delta, keys_part, values_part, allowed, scaling
):
    scores = tile_scores(queries, keys_part, allowed, scaling)
    probabilities = jnp.exp(scores - log_total[:, :, None])
    value_term = jnp.einsum(
        "hqk,qhd->khd",
        probabilities.astype(jnp.bfloat16),
        grad_rows,
        preferred_element_type=jnp.float32,
    )
    prob_grad = jnp.einsum(
        "qhd,khd->hqk", grad_rows, values_part, preferred_element_type=jnp.float32
    )
    score_grad = (probabilities * (prob_grad - row_delta[:, :, None])).astype(jnp.bfloat16)
    key_term = scaling * jnp.einsum(
        "hqk,qhd->khd", score_grad, queries, preferred_element_type=jnp.float32
    )
    return (key_term, value_term)


def shard_scan(step, carried, pieces, shard_rows):
    shard_total = pieces[0].shape[0] // shard_rows
    stacked = tuple(
        (member.reshape((shard_total, shard_rows) + member.shape[1:]) for member in pieces)
    )
    shard_ids = jnp.arange(shard_total, dtype=jnp.int32)

    def advance(current, element):
        return (step(current, element[1], element[0]), None)

    result, unused_out = lax.scan(advance, carried, (shard_ids, stacked))
    return result


def gather_plan(query_rows, key_rows, value_rows, out_grad, head_band, frame_map):
    shard_rows = query_rows.shape[0]
    head_count = query_rows.shape[1]
    head_width = query_rows.shape[2]
    frame_count = shard_rows // FRAME_TOK
    scaling = head_width ** (-0.5)
    own_index = lax.axis_index("ctx")
    own_frames = shard_frames(frame_map, own_index, frame_count)
    all_keys = lax.all_gather(key_rows, "ctx", axis=0, tiled=True)
    all_values = lax.all_gather(value_rows, "ctx", axis=0, tiled=True)

    def forward_step(carried, pieces, shard_id):
        allowed = frame_allowed(
            head_band, own_frames, shard_frames(frame_map, shard_id, frame_count)
        )

        def forward_compute(current):
            return forward_tile(current, query_rows, pieces[0], pieces[1], allowed, scaling)

        return lax.cond(jnp.any(allowed), forward_compute, keep_same, carried)

    start_state = (
        jnp.full((head_count, shard_rows), -1e30, jnp.float32),
        jnp.zeros((head_count, shard_rows), jnp.float32),
        jnp.zeros((shard_rows, head_count, head_width), jnp.float32),
    )
    forward_state = shard_scan(forward_step, start_state, (all_keys, all_values), shard_rows)
    run_max, run_sum, weighted = forward_state
    out_full = weighted / run_sum.T[:, :, None]
    attended = out_full.astype(jnp.bfloat16)
    log_total = run_max + jnp.log(run_sum)
    row_delta = jnp.sum(out_grad.astype(jnp.float32) * out_full, axis=2).T
    zero_rows = jnp.zeros((shard_rows, head_count, head_width), jnp.float32)

    def backward_step(carried, pieces, shard_id):
        allowed = frame_allowed(
            head_band, own_frames, shard_frames(frame_map, shard_id, frame_count)
        )

        def backward_compute(current):
            return current + query_grad_term(
                query_rows, out_grad, log_total, row_delta, pieces[0], pieces[1], allowed, scaling
            )

        return lax.cond(jnp.any(allowed), backward_compute, keep_same, carried)

    query_sum = shard_scan(backward_step, zero_rows, (all_keys, all_values), shard_rows)
    query_grad = (scaling * query_sum).astype(jnp.bfloat16)
    all_stats = (
        lax.all_gather(log_total, "ctx", axis=1, tiled=True),
        lax.all_gather(row_delta, "ctx", axis=1, tiled=True),
    )

    def key_step(carried, pieces, shard_id):
        allowed = frame_allowed(
            head_band, shard_frames(frame_map, shard_id, frame_count), own_frames
        )
        stat_log = lax.dynamic_slice_in_dim(all_stats[0], shard_id * shard_rows, shard_rows, 1)
        stat_delta = lax.dynamic_slice_in_dim(all_stats[1], shard_id * shard_rows, shard_rows, 1)

        def key_compute(current):
            key_term, value_term = key_grad_terms(
                pieces[0], pieces[1], stat_log, stat_delta, key_rows, value_rows, allowed, scaling
            )
            return (current[0] + narrowed(key_term), current[1] + narrowed(value_term))

        return lax.cond(jnp.any(allowed), key_compute, keep_same, carried)

    key_sum, value_sum = shard_scan(
        key_step,
        (zero_rows, zero_rows),
        (
            lax.all_gather(query_rows, "ctx", axis=0, tiled=True),
            lax.all_gather(out_grad, "ctx", axis=0, tiled=True),
        ),
        shard_rows,
    )
    key_grad = key_sum.astype(jnp.bfloat16)
    value_grad = value_sum.astype(jnp.bfloat16)
    return (attended, query_grad, key_grad, value_grad)


VMEM = pl.BlockSpec(memory_space=pltpu.VMEM)
SMEM = pl.BlockSpec(memory_space=pltpu.SMEM)
HBM = pl.BlockSpec(memory_space=pltpu.HBM)


def spread_body(slots, chunks, carried, own_ref, *refs):
    sources, refs = refs[:2], refs[2:]
    passenger, refs = (refs[0], refs[1:]) if carried else (None, refs)
    outs, (stage, wide, arrived) = refs[:slots], refs[slots:]
    rows, width = sources[0].shape
    part_rows = rows // chunks
    part_tokens = part_rows // slots
    own = own_ref[0]
    copies = [
        pltpu.make_async_copy(
            source.at[pl.ds(chunk * part_rows, part_rows), :],
            stage.at[which, pl.ds(chunk * part_rows, part_rows), :],
            arrived.at[which, chunk],
        )
        for which, source in enumerate(sources)
        for chunk in range(chunks)
    ]
    for copy in copies:
        copy.start()
    if carried:
        outs[1][:, 2 * width :] = passenger[...]
    for step, copy in enumerate(copies):
        which, chunk = divmod(step, chunks)
        first = chunk * part_rows
        copy.wait()
        wide[which, first : first + part_rows, :] = stage[
            which, first : first + part_rows, :
        ].astype(jnp.float32)
        tokens = slice(chunk * part_tokens, (chunk + 1) * part_tokens)
        for slot in range(slots):
            picked = wide[which, pl.ds(first + (own ^ slot), part_tokens, stride=slots), :]
            outs[slot][tokens, which * width : (which + 1) * width] = picked.astype(jnp.bfloat16)


def spread(own, first, second, passenger=None, chunks=4):
    tokens, slots, width = first.shape
    rows = tokens * slots
    shapes = [jax.ShapeDtypeStruct((tokens, 2 * width), jnp.bfloat16)] * slots
    operands = [own] + [
        pltpu.with_memory_space_constraint(array.reshape(rows, width), pltpu.HBM)
        for array in (first, second)
    ]
    specs = [SMEM, HBM, HBM]
    if passenger is not None:
        operands.append(passenger)
        specs.append(VMEM)
        shapes[1] = jax.ShapeDtypeStruct((tokens, 4 * width), jnp.bfloat16)
    return list(
        pl.pallas_call(
            functools.partial(spread_body, slots, chunks, passenger is not None),
            out_shape=shapes,
            in_specs=specs,
            out_specs=[VMEM] * slots,
            scratch_shapes=[
                pltpu.VMEM((2, rows, width), jnp.bfloat16),
                pltpu.VMEM((2, rows, width), jnp.float32),
                pltpu.SemaphoreType.DMA((2, chunks)),
            ],
            cost_estimate=pl.CostEstimate(
                flops=0, transcendentals=0, bytes_accessed=8 * rows * width
            ),
            compiler_params=pltpu.CompilerParams(vmem_limit_bytes=12 << 20),
            name="spread",
        )(*operands)
    )


def collect_body(slots, starts, chunks, own_ref, *refs):
    pieces, targets, (wide, stage, left) = refs[:slots], refs[slots:-3], refs[-3:]
    rows, width = targets[0].shape
    part_rows = rows // chunks
    part_tokens = part_rows // slots
    own = own_ref[0]
    copies = []
    for which, target in enumerate(targets):
        for chunk in range(chunks):
            first = chunk * part_rows
            tokens = slice(chunk * part_tokens, (chunk + 1) * part_tokens)
            for slot in range(slots):
                start = starts[slot] + which * width
                piece = pieces[slot][tokens, start : start + width].astype(jnp.float32)
                wide[which, pl.ds(first + (own ^ slot), part_tokens, stride=slots), :] = piece
            stage[which, first : first + part_rows, :] = wide[
                which, first : first + part_rows, :
            ].astype(jnp.bfloat16)
            copy = pltpu.make_async_copy(
                stage.at[which, pl.ds(first, part_rows), :],
                target.at[pl.ds(first, part_rows), :],
                left.at[which, chunk],
            )
            copy.start()
            copies.append(copy)
    for copy in copies:
        copy.wait()


def collect(own, pieces, starts, chunks=8):
    slots = len(pieces)
    tokens, width = pieces[0].shape[0], pieces[0].shape[1] // 2
    rows = tokens * slots
    first, second = pl.pallas_call(
        functools.partial(collect_body, slots, starts, chunks),
        out_shape=[jax.ShapeDtypeStruct((rows, width), jnp.bfloat16)] * 2,
        in_specs=[SMEM] + [VMEM] * slots,
        out_specs=[HBM] * 2,
        scratch_shapes=[
            pltpu.VMEM((2, rows, width), jnp.float32),
            pltpu.VMEM((2, rows, width), jnp.bfloat16),
            pltpu.SemaphoreType.DMA((2, chunks)),
        ],
        cost_estimate=pl.CostEstimate(flops=0, transcendentals=0, bytes_accessed=8 * rows * width),
        compiler_params=pltpu.CompilerParams(vmem_limit_bytes=12 << 20),
        name="collect",
    )(own, *pieces)
    return first.reshape(tokens, slots, width), second.reshape(tokens, slots, width)


def join_body(slots, *refs):
    pieces, (rows_ref, flat_ref) = refs[:slots], refs[slots:]
    tokens = pieces[0].shape[0]
    both = rows_ref.shape[1]
    for slot in range(slots):
        piece = pieces[slot][:, pieces[slot].shape[1] - both :]
        rows_ref[slot * tokens : (slot + 1) * tokens, :] = piece
        flat_ref[:, slot * tokens : (slot + 1) * tokens] = piece.T


def join(pieces):
    slots = len(pieces)
    tokens, both = pieces[0].shape
    return pl.pallas_call(
        functools.partial(join_body, slots),
        out_shape=[
            jax.ShapeDtypeStruct((slots * tokens, both), jnp.bfloat16),
            jax.ShapeDtypeStruct((both, slots * tokens), jnp.bfloat16),
        ],
        in_specs=[VMEM] * slots,
        out_specs=[VMEM] * 2,
        cost_estimate=pl.CostEstimate(
            flops=0, transcendentals=0, bytes_accessed=6 * slots * tokens * both
        ),
        compiler_params=pltpu.CompilerParams(vmem_limit_bytes=12 << 20),
        name="join",
    )(*pieces)


def attend_body(
    slots, slot, first, last, own_ref, band_ref, map_ref, qg_ref, kv_ref, kvt_ref, *rest
):
    if first:
        sums_in = None
    else:
        sums_in, rest = rest[0], rest[1:]
    if last:
        passenger, rest = rest[0], rest[1:]
    out_ref, rest = rest[0], rest[1:]
    if last:
        parts, rest = rest[:slots], rest[slots:]
        sums_ref, rest = rest[0], rest[1:]
        parts[1][:, kv_ref.shape[1] :] = passenger[...]
    else:
        sums_ref, rest = rest[0], rest[1:]
    scores_ref, out_acc, grad_acc = rest
    tokens = qg_ref.shape[0]
    width = kv_ref.shape[1] // 2
    frames = tokens // FRAME_TOK
    keys = kv_ref.shape[0]
    scaling = width ** (-0.5)
    power = scaling * math.log2(math.e)
    own = own_ref[0]

    queries = qg_ref[:, :width]
    grads = qg_ref[:, width : 2 * width]
    queries_t = queries.T
    grads_t = grads.T
    lane = lax.broadcasted_iota(jnp.int32, (1, tokens), 1)

    def allowed_row(tile):
        key_frame = map_ref[(own ^ (tile // frames)) * frames + tile % frames]
        row = jnp.zeros((1, tokens), jnp.int32)
        for frame in range(frames):
            gap = jnp.abs(map_ref[(own ^ slot) * frames + frame] - key_frame)
            row = jnp.where(lane // FRAME_TOK == frame, band_ref[own, gap], row)
        return row == 1

    def tile_rows(tile):
        return pl.ds(pl.multiple_of(tile * FRAME_TOK, FRAME_TOK), FRAME_TOK)

    def score_step(tile, row_max):
        rows = tile_rows(tile)
        scores = jnp.dot(kv_ref[rows, :width], queries_t, preferred_element_type=jnp.float32)
        scores_ref[rows, :] = scores
        tile_max = jnp.max(scores, axis=0, keepdims=True)
        return jnp.maximum(row_max, jnp.where(allowed_row(tile), tile_max, -jnp.inf))

    tiles = keys // FRAME_TOK
    row_max = lax.fori_loop(0, tiles, score_step, jnp.full((1, tokens), -jnp.inf, jnp.float32), unroll=8)
    row_max = row_max * power
    out_acc[...] = jnp.zeros_like(out_acc)

    def weight_step(tile, total):
        rows = tile_rows(tile)
        shift = jnp.where(allowed_row(tile), row_max, jnp.inf)
        weights = jnp.exp2(scores_ref[rows, :] * power - shift)
        scores_ref[rows, :] = weights
        out_acc[...] += jnp.dot(
            kvt_ref[width:, rows], weights.astype(jnp.bfloat16), preferred_element_type=jnp.float32
        )
        return total + jnp.sum(weights, axis=0, keepdims=True)

    total = lax.fori_loop(0, tiles, weight_step, jnp.zeros((1, tokens), jnp.float32), unroll=8)
    inverse = 1.0 / total
    out_full = out_acc[...] * inverse
    delta = jnp.sum(out_full * grads_t.astype(jnp.float32), axis=0, keepdims=True)
    out_ref[:, :width] = out_full.T.astype(jnp.bfloat16)
    grad_acc[...] = jnp.zeros_like(grad_acc)

    def grad_step(tile, carried):
        rows = tile_rows(tile)
        probabilities = scores_ref[rows, :] * inverse
        prob_grad = jnp.dot(kv_ref[rows, width:], grads_t, preferred_element_type=jnp.float32)
        score_grad = (probabilities * (prob_grad - delta)).astype(jnp.bfloat16)
        value_term = jnp.dot(
            probabilities.astype(jnp.bfloat16), grads, preferred_element_type=jnp.float32
        )
        key_term = jnp.dot(score_grad, queries, preferred_element_type=jnp.float32)
        grad_acc[...] += jnp.dot(
            kvt_ref[:width, rows], score_grad, preferred_element_type=jnp.float32
        )
        if first:
            sums_ref[rows, :width] = key_term
            sums_ref[rows, width:] = value_term
        else:
            sums_ref[rows, :width] = sums_in[rows, :width] + key_term
            sums_ref[rows, width:] = sums_in[rows, width:] + value_term
        return carried

    lax.fori_loop(0, tiles, grad_step, 0, unroll=8)
    out_ref[:, width:] = (grad_acc[...] * scaling).T.astype(jnp.bfloat16)
    if last:
        for part in range(slots):
            rows = slice(part * tokens, (part + 1) * tokens)
            parts[part][:, :width] = (sums_ref[rows, :width] * scaling).astype(jnp.bfloat16)
            parts[part][:, width : 2 * width] = sums_ref[rows, width:].astype(jnp.bfloat16)


def attend(slots, slot, first, last, own, head_band, frame_map, pair, kv, kvt, sums, passenger=None):
    tokens, both = pair.shape[0], kv.shape[1]
    keys, width = kv.shape[0], both // 2
    piece = jax.ShapeDtypeStruct((tokens, both), jnp.bfloat16)
    sums_shape = jax.ShapeDtypeStruct((keys, both), jnp.float32)
    outs = [piece] + ([piece] * slots if last else [sums_shape])
    if last:
        outs[2] = jax.ShapeDtypeStruct((tokens, 2 * both), jnp.bfloat16)
    scratch = [
        pltpu.VMEM((keys, tokens), jnp.float32),
        pltpu.VMEM((width, tokens), jnp.float32),
        pltpu.VMEM((width, tokens), jnp.float32),
    ]
    if last:
        scratch = [pltpu.VMEM((keys, both), jnp.float32)] + scratch
    operands = [own, head_band, frame_map, pair, kv, kvt] + ([] if first else [sums])
    if last:
        operands.append(passenger)
    return pl.pallas_call(
        functools.partial(attend_body, slots, slot, first, last),
        out_shape=outs,
        in_specs=[SMEM] * 3 + [VMEM] * (len(operands) - 3),
        out_specs=[VMEM] * len(outs),
        scratch_shapes=scratch,
        input_output_aliases={} if first or last else {6: 1},
        cost_estimate=pl.CostEstimate(
            flops=12 * tokens * keys * width,
            transcendentals=tokens * keys,
            bytes_accessed=10 * keys * both,
        ),
        compiler_params=pltpu.CompilerParams(vmem_limit_bytes=24 << 20),
        name="attend",
    )(*operands)


def exchange_plan(slots, query_rows, key_rows, value_rows, out_grad, head_band, frame_map):
    own_index = lax.axis_index("ctx").astype(jnp.int32)
    own = own_index.reshape(1)

    def swap(piece, slot):
        return lax.ppermute(piece, "ctx", [(place, place ^ slot) for place in range(slots)])

    def after(values, *gates):
        return lax.optimization_barrier((values, gates))[0]

    kv_slots = spread(own, key_rows, value_rows)
    qg_slots = spread(own, query_rows, out_grad)
    for slot in range(1, slots):
        kv_slots[slot] = swap(kv_slots[slot], slot)
    qg_slots[1] = swap(qg_slots[1], 1)
    kv, kvt = join(kv_slots)
    both = kv.shape[1]
    back = list(kv_slots)
    gate = kv_slots[2]
    sums = None
    for slot in range(slots):
        last = slot == slots - 1
        if slot + 2 < slots:
            qg_slots[slot + 2] = swap(after(qg_slots[slot + 2], gate), slot + 2)
        results = attend(
            slots, slot, slot == 0, last, own, head_band, frame_map, qg_slots[slot], kv, kvt, sums,
            back[1],
        )
        back[slot] = results[0] if slot < 2 else swap(results[0], slot)
        sums = results[1]
        gate = results[0]
    grads = list(results[1:])
    grads[2:] = after(grads[2:], back[2])
    grads = [swap(part, slot) if slot else part for slot, part in enumerate(grads)]
    back[1] = grads[1]
    attended, query_grad = collect(own, back, [both if slot == 1 else 0 for slot in range(slots)])
    grads = after(grads, attended)
    key_grad, value_grad = collect(own, grads, [0] * slots)
    return (attended, query_grad, key_grad, value_grad)


def solution(mesh):
    slots = mesh.shape["ctx"]

    def on_device(query_rows, *others):
        if query_rows.shape[1] == slots >= 4 and slots & (slots - 1) == 0:
            return exchange_plan(slots, query_rows, *others)
        return gather_plan(query_rows, *others)

    rows = P(("groups", "ctx"), ("head", "aux"), None)
    return jax.shard_map(
        on_device,
        mesh=mesh,
        in_specs=(rows, rows, rows, rows, P(("head", "aux"), None), P()),
        out_specs=(rows, rows, rows, rows),
        check_vma=False,
    )
```
